128 devices in a mesh: seq: 32 (over z, x, core), head: 4 (over y).
Axes of the slice: x: 4, y: 4, z: 4, core: 2. Of those that a mesh axis runs over, the one named last changes fastest.
Arguments:
- queries: bfloat16 [16384, 4096], P('seq', 'head'), may hold values from -24 to 24
- key_states: bfloat16 [16384, 4096], P('seq', 'head'), may hold values from -24 to 24
- value_states: bfloat16 [16384, 4096], P('seq', 'head'), may hold values from -6 to 6
- forward_out: bfloat16 [16384, 4096], P('seq', 'head'), may hold values from -3 to 3
- grad_out: bfloat16 [16384, 4096], P('seq', 'head'), may hold values from -96 to 96
- random_blocks: int32 [256, 32, 3], P(None, 'head'), may hold values from 0 to 255, as said below
- global_blocks: int32 [2], replicated, may hold values from 0 to 255, as said below
Outputs:
- grad_queries: bfloat16 [16384, 4096], P(('seq', 'head'))
- grad_keys: bfloat16 [16384, 4096], P(('seq', 'head'))
- grad_values: bfloat16 [16384, 4096], P(('seq', 'head'))
The draws below stay inside these ranges and needn't reach their ends.
Inputs may be any that keep to these rules, and one draw needn't show every extreme that they name: `random_blocks`: for the query blocks of one shard of 512 tokens and the 8 heads of one head group, at most 8 of the 192 entries name blocks held by any one shard of 8 blocks, and one shard, the same for every group, is named exactly 8 times by every group. `global_blocks`: two different blocks, one of them the last block 255.
All inputs are finite; a program needn't handle non-finite values.
Results may differ from the reference program's by a relative error of at most 0.0053.
Values may be sent and summed in bfloat16 or wider, within the bound.
A program may use at most 128 MiB of HBM per device.

```python
import jax
import jax.numpy as jnp
from jax import lax

HEADS = 32
DH = 128
BS = 64
HD = 8
QB_DEV = 8
NB = 256
SEQ = 16384
REQUESTS = 192
SLOTS = 8


def draw_pair(key):
    base = jax.random.fold_in(key, 7)
    key_query, key_keys = jax.random.split(base, 2)
    shape = (SEQ, HEADS * DH)
    query_draw = jax.random.truncated_normal(key_query, -6.0, 6.0, shape, jnp.float32)
    keys_draw = jax.random.truncated_normal(key_keys, -6.0, 6.0, shape, jnp.float32)
    return (query_draw, keys_draw)


def draw_queries(key, part):
    return draw_pair(key)[0].astype(jnp.bfloat16)


def draw_key_states(key, part):
    return draw_pair(key)[1].astype(jnp.bfloat16)


def draw_random_blocks(key, part):
    seq_count = NB // QB_DEV
    group_count = HEADS // HD
    key_hot, key_groups = jax.random.split(jax.random.fold_in(key, 11))
    hot_owner = jax.random.randint(key_hot, (), 0, seq_count)

    def one_group(group_key):
        key_pool, key_order, key_local = jax.random.split(group_key, 3)
        others = jnp.arange(seq_count - 1, dtype=jnp.int32)
        others = others + (others >= hot_owner).astype(jnp.int32)
        pool = jnp.repeat(others, SLOTS, total_repeat_length=(seq_count - 1) * SLOTS)
        pool = jax.random.permutation(key_pool, pool)[:REQUESTS - SLOTS]
        owners = jnp.concatenate([jnp.full((SLOTS,), hot_owner, jnp.int32), pool])
        owners = jax.random.permutation(key_order, owners)
        local_block = jax.random.randint(key_local, (REQUESTS,), 0, QB_DEV)
        return (owners * QB_DEV + local_block).astype(jnp.int32)
    group_keys = jax.random.split(key_groups, seq_count * group_count)
    table = jax.vmap(one_group)(group_keys)
    table = table.reshape(seq_count, group_count, QB_DEV, HD, 3).transpose(0, 2, 1, 3, 4)
    return table.reshape(NB, HEADS, 3)


def draw_global_blocks(key, part):
    key_other, key_flip = jax.random.split(jax.random.fold_in(key, 13))
    other_block = jax.random.randint(key_other, (), 0, NB - 1).astype(jnp.int32)
    last_block = jnp.full((), NB - 1, jnp.int32)
    flip = jax.random.randint(key_flip, (), 0, 2)
    first = jnp.where(flip == 0, other_block, last_block)
    second = jnp.where(flip == 0, last_block, other_block)
    return jnp.stack([first, second]).astype(jnp.int32)


def block_scale(own_key, extent, shards, low, largest):
    gain, own = 1.0, jax.random.fold_in(own_key, 6)
    for position, shards_of in shards:
        heights = jnp.exp(jax.random.uniform(jax.random.fold_in(own, position), (shards_of,), jnp.float32, low / len(shards), largest / len(shards)))
        gain = gain * jnp.repeat(heights, extent[position] // shards_of).reshape([-1 if axis == position else 1 for axis in range(len(extent))])
    return gain


def bell_draw(rng, shape, width, bound, pieces=(), held_as=jnp.bfloat16):
    loudness = block_scale(rng, shape, pieces, -0.22, 0.18) if pieces else 1.0
    entries = jax.random.normal(rng, shape, jnp.float32) * width * loudness
    return jnp.minimum(jnp.maximum(entries, -bound), bound).astype(held_as)


def setup_inputs(seed: int = 0) -> dict:
    arg_keys = jax.random.split(jax.random.key(seed), 8)
    return {
        "queries": draw_queries(jax.random.fold_in(arg_keys[7], 71), 0),
        "key_states": draw_key_states(jax.random.fold_in(arg_keys[7], 71), 0),
        "value_states": bell_draw(arg_keys[2], (SEQ, HEADS * DH), 1.0, 6.0, ((0, 32), (1, 4))),
        "forward_out": bell_draw(arg_keys[3], (SEQ, HEADS * DH), 0.5, 3.0, ((0, 32), (1, 4))),
        "grad_out": bell_draw(arg_keys[4], (SEQ, HEADS * DH), 16.0, 96.0, ((0, 32), (1, 4))),
        "random_blocks": draw_random_blocks(jax.random.fold_in(arg_keys[7], 71), 0),
        "global_blocks": draw_global_blocks(jax.random.fold_in(arg_keys[7], 71), 0),
    }


def round_trip(values):
    return lax.optimization_barrier(values.astype(jnp.bfloat16)).astype(jnp.float32)


def split_heads(array):
    return array.reshape(-1, BS, HEADS, DH).transpose(2, 0, 1, 3)


def merge_heads(array):
    return array.transpose(1, 2, 0, 3).reshape(-1, HEADS * DH)


def head_grads(operands, global_blocks):
    query_row_block, key_rows, value_rows, saved_rows, gradient_row_block, chosen = operands
    block_count = query_row_block.shape[0]
    softmax_scale = DH ** -0.5
    zero_block = jnp.zeros_like(key_rows[:1])

    def listed(rows):
        padded = jnp.concatenate([zero_block, rows, zero_block], axis=0)
        window_set = jnp.stack([padded[:-2], padded[1:-1], padded[2:]], axis=1)
        random_set = rows[chosen]
        global_set = jnp.broadcast_to(rows[global_blocks][None], (block_count, 2, BS, DH))
        return jnp.concatenate([window_set, random_set, global_set], axis=1).astype(jnp.float32)

    gathered_key_block = listed(key_rows)
    gathered_value_block = listed(value_rows)
    block_ids = jnp.arange(block_count)
    always = jnp.ones((block_count,), bool)
    usable = jnp.stack([block_ids > 0, always, block_ids < block_count - 1, always, always, always, always, always], axis=1)
    query_float32 = query_row_block.astype(jnp.float32)
    gradient_float32 = gradient_row_block.astype(jnp.float32)
    logit_scores = softmax_scale * jnp.einsum("zxp,zufp->zxuf", query_float32, gathered_key_block)
    logit_scores = jnp.where(usable[:, None, :, None], logit_scores, -jnp.inf)
    peak_score = jnp.max(logit_scores, axis=(2, 3))
    row_sum = jnp.sum(jnp.exp(logit_scores - peak_score[:, :, None, None]), axis=(2, 3))
    log_norm = peak_score + jnp.log(row_sum)
    weights = jnp.exp(logit_scores - log_norm[:, :, None, None])
    row_dot = jnp.sum(gradient_float32 * saved_rows.astype(jnp.float32), axis=-1)
    weight_gradient = jnp.einsum("zxp,zufp->zxuf", gradient_float32, gathered_value_block)
    dscores = weights * (weight_gradient - row_dot[:, :, None, None])
    weight_lowp = round_trip(weights)
    score_gradient_lowp = round_trip(dscores)
    dq_terms = softmax_scale * jnp.einsum("bqjk,bjkd->bqjd", score_gradient_lowp, gathered_key_block)
    key_gradient_parts = softmax_scale * jnp.einsum("rmnf,rmc->rnfc", score_gradient_lowp, query_float32)
    value_gradient_parts = jnp.einsum("rmnf,rmc->rnfc", weight_lowp, gradient_float32)
    grad_query = jnp.sum(dq_terms[:, :, :3], axis=2) + jnp.sum(dq_terms[:, :, 6:], axis=2)
    grad_query = grad_query + jnp.sum(round_trip(dq_terms[:, :, 3:6]), axis=2)

    def key_side(slot_terms):
        zero_term = jnp.zeros_like(slot_terms[:1, 0])
        gathered = slot_terms[:, 1] + jnp.concatenate([slot_terms[1:, 0], zero_term], axis=0)
        gathered = gathered + jnp.concatenate([zero_term, slot_terms[:-1, 2]], axis=0)
        gathered = gathered.at[chosen.reshape(-1)].add(round_trip(slot_terms[:, 3:6]).reshape(-1, BS, DH))
        gathered = gathered.at[global_blocks].add(jnp.sum(slot_terms[:, 6:], axis=0))
        return gathered.astype(jnp.bfloat16)

    return grad_query.astype(jnp.bfloat16), key_side(key_gradient_parts), key_side(value_gradient_parts)


def reference(queries, key_states, value_states, forward_out, grad_out, random_blocks, global_blocks):
    operands = (split_heads(queries), split_heads(key_states), split_heads(value_states),
                split_heads(forward_out), split_heads(grad_out), random_blocks.transpose(1, 0, 2))
    grad_q, grad_k, grad_v = lax.map(lambda inputs: head_grads(inputs, global_blocks), operands)
    return merge_heads(grad_q), merge_heads(grad_k), merge_heads(grad_v)
```

```python
import jax
import jax.numpy as jnp
from jax import lax
from jax.experimental import pallas as pl
from jax.experimental.pallas import tpu as pltpu
from jax.sharding import PartitionSpec as P

DH = 128
BS = 64
SCALE = DH**-0.5
X_GROUPS = [[z * 8 + x * 2 + c for x in range(4)] for z in range(4) for c in range(2)]
HEAD_GROUPS = [
    [(2 * zh + zl) * 8 + x * 2 + c for zl in range(2) for c in range(2)]
    for zh in range(2)
    for x in range(4)
]
MIRROR = [(s, (3 - s // 8) * 8 + s % 8) for s in range(32)]
NT = (((1,), (1,)), ((), ()))
TN = (((0,), (0,)), ((), ()))


def dot(a, b, dims):
    return lax.dot_general(a, b, dims, preferred_element_type=jnp.float32)


def attend_kernel(tab, edge, q_ref, g_ref, rd_ref, kv_ref, dq_ref, dkv_ref, acc_ref):
    acc_ref[...] = jnp.zeros_like(acc_ref)
    lane = lax.broadcasted_iota(jnp.int32, (1, 8 * BS), 1)
    eye = lax.broadcasted_iota(jnp.int32, (BS, BS), 0) == lax.broadcasted_iota(
        jnp.int32, (BS, BS), 1
    )

    def step(i, carry):
        slots = [tab[i * 8 + j] for j in range(8)]
        keys = jnp.concatenate([kv_ref[p] for p in slots], axis=0)
        values = jnp.concatenate([kv_ref[p + 8] for p in slots], axis=0)
        q = q_ref[i]
        g = g_ref[i]
        state = edge[i]
        gone = ((lane < BS) & (state == 1)) | (
            (lane >= 2 * BS) & (lane < 3 * BS) & (state == 2)
        )
        bias = jnp.where(gone, -jnp.inf, 0.0)
        scores = dot(q, keys, NT) * SCALE + bias
        peak = jnp.max(scores, axis=1, keepdims=True)
        e = jnp.exp(scores - peak)
        weights = e * (1.0 / jnp.sum(e, axis=1, keepdims=True))
        rd = jnp.sum(jnp.where(eye, rd_ref[pl.ds(i, 1), :], 0.0), axis=1, keepdims=True)
        ds = weights * (dot(g, values, NT) - rd)
        wb = weights.astype(jnp.bfloat16)
        dsb = ds.astype(jnp.bfloat16)
        dq_ref[i] = (dot(dsb, keys, (((1,), (0,)), ((), ()))) * SCALE).astype(jnp.bfloat16)
        dk = dot(dsb, q, TN) * SCALE
        dv = dot(wb, g, TN)
        for j, p in enumerate(slots):
            acc_ref[p] += dk[j * BS : (j + 1) * BS]
            acc_ref[p + 8] += dv[j * BS : (j + 1) * BS]
        return carry

    lax.fori_loop(0, 64, step, 0)
    dkv_ref[...] = acc_ref[...].astype(jnp.bfloat16)


def attend(tab, edge, q, g, rd, kv):
    vmem = pl.BlockSpec(memory_space=pltpu.VMEM)
    smem = pl.BlockSpec(memory_space=pltpu.SMEM)
    return pl.pallas_call(
        attend_kernel,
        out_shape=(
            jax.ShapeDtypeStruct((64, BS, DH), jnp.bfloat16),
            jax.ShapeDtypeStruct((512, BS, DH), jnp.bfloat16),
        ),
        in_specs=[smem, smem, vmem, vmem, vmem, vmem],
        out_specs=(vmem, vmem),
        scratch_shapes=[pltpu.VMEM((512, BS, DH), jnp.float32)],
        compiler_params=pltpu.CompilerParams(vmem_limit_bytes=60 * 1024 * 1024),
    )(tab, edge, q, g, rd, kv)


def place(block, zhi):
    z, x, c = block // 64, block // 16 % 4, block // 8 % 2
    near = z // 2 == zhi
    zlo = jnp.where(near, z % 2, (3 - z) % 2)
    slot = ((zlo * 2 + c) * 2 + jnp.where(near, 0, 1)) * 4 + x
    return slot * 16 + block % 8


def tables(random_blocks, global_blocks, z, x, c):
    zhi = z // 2
    mine = lax.dynamic_index_in_dim(random_blocks, x * 2 + zhi, 1, keepdims=False)
    mine = mine.reshape(4, 4, 2, 8, 3)
    mine = lax.dynamic_index_in_dim(mine, c, 2, keepdims=False)
    near = lax.dynamic_index_in_dim(mine, z, 0, keepdims=False)
    far = lax.dynamic_index_in_dim(mine, 3 - z, 0, keepdims=False)
    rand = jnp.stack([near, far]).reshape(64, 3)
    ids = jnp.arange(64, dtype=jnp.int32)
    zs = jnp.where(ids < 32, z, 3 - z)
    block = zs * 64 + ids // 8 % 4 * 16 + c * 8 + ids % 8
    window = jnp.stack([block - 1, block, block + 1], axis=1)
    window = jnp.clip(window, 0, 255)
    globs = jnp.broadcast_to(global_blocks[None], (64, 2))
    table = place(jnp.concatenate([window, rand, globs], axis=1), zhi)
    edge = jnp.where(block == 0, 1, jnp.where(block == 255, 2, 0))
    return table.reshape(512), edge


def on_device(
    queries, key_states, value_states, forward_out, grad_out, random_blocks, global_blocks
):
    s = lax.axis_index("seq")
    z, x, c = s // 8, s // 2 % 4, s % 2
    zhi = z // 2
    tab, edge = tables(random_blocks, global_blocks, z, x, c)
    row_dot = jnp.sum(
        (grad_out.astype(jnp.float32) * forward_out.astype(jnp.float32)).reshape(512, 8, DH),
        axis=2,
    )

    def over_x(a):
        return lax.all_to_all(a, "seq", 0, 0, axis_index_groups=X_GROUPS, tiled=True)

    def to_head(a):
        own = lax.dynamic_index_in_dim(a, zhi, 0, keepdims=False)
        other = lax.dynamic_index_in_dim(a, 1 - zhi, 0, keepdims=False)
        return jnp.stack([own, lax.ppermute(other, "seq", MIRROR)])

    kv = jnp.stack([key_states, value_states]).reshape(2, 512, 4, 2, DH).transpose(2, 3, 0, 1, 4)
    kv = to_head(over_x(kv).transpose(1, 0, 2, 3, 4))
    kv = lax.all_gather(kv, "seq", axis_index_groups=HEAD_GROUPS)
    qg = jnp.stack([queries, grad_out]).reshape(2, 512, 4, 2, DH).transpose(2, 3, 0, 1, 4)
    qg = to_head(over_x(qg).transpose(1, 2, 0, 3, 4))
    rd = to_head(over_x(row_dot.T.reshape(4, 2, 512)).transpose(1, 0, 2))
    dq, dkv = attend(
        tab,
        edge,
        qg[:, 0].reshape(64, BS, DH),
        qg[:, 1].reshape(64, BS, DH),
        rd.reshape(64, BS),
        kv.reshape(512, BS, DH),
    )
    dkv = lax.psum_scatter(
        dkv.reshape(4, 2, 4, 2, 512, DH), "seq", axis_index_groups=HEAD_GROUPS
    )
    full = jnp.concatenate([dq.reshape(2, 4, 1, 512, DH), dkv], axis=2)
    near, far = full[0], lax.ppermute(full[1], "seq", MIRROR)
    low = zhi == 0
    both = jnp.stack([jnp.where(low, near, far), jnp.where(low, far, near)], axis=3)
    rows = over_x(both.reshape(4, 3, 512, 2 * DH)).transpose(1, 2, 0, 3).reshape(3, 512, 1024)
    outs = lax.all_to_all(rows, "head", split_axis=1, concat_axis=2, tiled=True)
    return outs[0], outs[1], outs[2]


def solution(mesh):
    return jax.shard_map(
        on_device,
        mesh=mesh,
        in_specs=(
            P("seq", "head"),
            P("seq", "head"),
            P("seq", "head"),
            P("seq", "head"),
            P("seq", "head"),
            P(None, "head", None),
            P(),
        ),
        out_specs=(P(("seq", "head"), None), P(("seq", "head"), None), P(("seq", "head"), None)),
        check_vma=False,
    )
```

```python
import jax
import jax.numpy as jnp
from jax import lax
from jax.experimental import pallas as pl
from jax.experimental.pallas import tpu as pltpu
from jax.sharding import PartitionSpec as P

DH = 128
BS = 64
SCALE = DH**-0.5
X_GROUPS = [[z * 8 + x * 2 + c for x in range(4)] for z in range(4) for c in range(2)]
HEAD_GROUPS = [
    [(2 * zh + zl) * 8 + x * 2 + c for zl in range(2) for c in range(2)]
    for zh in range(2)
    for x in range(4)
]
MIRROR = [(s, (3 - s // 8) * 8 + s % 8) for s in range(32)]
NT = (((1,), (1,)), ((), ()))
TN = (((0,), (0,)), ((), ()))


def dot(a, b, dims):
    return lax.dot_general(a, b, dims, preferred_element_type=jnp.float32)


MESH = pl.DeviceIdType.MESH


def fetch_kernel(
    k_ref, v_ref, q_ref, g_ref, rd_ref,
    kv_out, qg_out, rdx, rdm,
    loc, oth, hop,
    send, local, from_x, from_2, from_hop, from_pair, from_mirror, from_core, from_rd,
):
    s = lax.axis_index("seq")
    z, x, c = s // 8, s // 2 % 4, s % 2
    zhi = z // 2
    mirror, pair, core = 3 - z, z + 1 - 2 * (z % 2), 1 - c

    def index(zz, xx, cc):
        return zz * 8 + xx % 4 * 2 + cc

    to_mirror, to_pair, to_core = index(mirror, x, c), index(pair, x, c), index(z, x, core)
    barrier = pltpu.get_barrier_semaphore()
    greet = [index(z, x + d, c) for d in (1, 2, 3)] + [to_mirror, to_pair, to_core]
    for peer in greet:
        pl.semaphore_signal(barrier, inc=1, device_id={"seq": peer}, device_id_type=MESH)
    pl.semaphore_wait(barrier, len(greet))

    sends = []

    def push(src, dst, sem, peer):
        copy = pltpu.make_async_remote_copy(
            src_ref=src,
            dst_ref=dst,
            send_sem=send.at[len(sends)],
            recv_sem=sem,
            device_id={"seq": peer},
            device_id_type=MESH,
        )
        copy.start()
        sends.append(copy)

    def arrived(dst, sem):
        pltpu.make_async_remote_copy(
            src_ref=dst,
            dst_ref=dst,
            send_sem=send.at[0],
            recv_sem=sem,
            device_id={"seq": to_core},
            device_id_type=MESH,
        ).wait_recv()

    locals_ = []

    def move(src, dst):
        copy = pltpu.make_async_copy(src, dst, local.at[len(locals_)])
        copy.start()
        locals_.append(copy)
        return copy

    ins = (k_ref, v_ref, q_ref, g_ref)

    def own(a, xx):
        return ins[a].at[:, pl.ds(pl.multiple_of(xx % 4 * 256 + zhi * DH, DH), DH)]

    def other(a, xx):
        return ins[a].at[:, pl.ds(pl.multiple_of(xx % 4 * 256 + (1 - zhi) * DH, DH), DH)]

    def own_slot(a, src_s, src_x):
        return kv_out.at[src_s, a] if a < 2 else qg_out.at[src_x, a - 2]

    def send_x(arrays):
        for a in arrays:
            push(own(a, x + 2), hop.at[0, a], from_hop.at[0, a], index(z, x + 1, c))
            push(other(a, x + 2), hop.at[1, a], from_hop.at[1, a], index(z, x + 3, c))
            for d in (1, 3):
                peer = index(z, x + d, c)
                push(own(a, x + d), own_slot(a, s, x), from_x.at[d // 2, a, 0], peer)
                push(other(a, x + d), oth.at[x, a], from_x.at[d // 2, a, 1], peer)

    def relay(pair_of, base):
        for a in pair_of:
            arrived(hop.at[0, a], from_hop.at[0, a])
        left, right = (x + 3) % 4, (x + 1) % 4
        both = pl.ds(base, 2)
        dst = kv_out.at[index(z, left, c)] if base == 0 else qg_out.at[left]
        push(hop.at[0, both], dst, from_2.at[base], index(z, right, c))
        for a in pair_of:
            arrived(hop.at[1, a], from_hop.at[1, a])
        push(hop.at[1, both], oth.at[right, both], from_2.at[base + 1], index(z, left, c))

    loads = [[move(own(a, x), loc.at[a]), move(other(a, x), oth.at[x, a])] for a in range(4)]
    rd_load = move(rd_ref.at[x], rdx.at[x])
    send_x((0, 1))
    for d in (1, 2, 3):
        push(rd_ref.at[(x + d) % 4], rdx.at[x], from_rd.at[d], index(z, x + d, c))
    for a in (0, 1):
        loads[a][0].wait()
        loads[a][1].wait()
    kv = pl.ds(0, 2)
    qg = pl.ds(2, 2)
    push(loc.at[kv], kv_out.at[s], from_pair.at[0, 0], to_pair)
    push(oth.at[x, kv], kv_out.at[s], from_mirror.at[0, 0], to_mirror)
    push(loc.at[kv], kv_out.at[s], from_core.at[0, 0], to_core)
    stores = [move(loc.at[kv], kv_out.at[s])]
    send_x((2, 3))
    for a in (2, 3):
        loads[a][0].wait()
        loads[a][1].wait()
    stores.append(move(loc.at[qg], qg_out.at[x]))
    relay((0, 1), 0)
    for r in (3, 1, 2):
        src = (x + r) % 4
        slot = index(z, src, c)
        if r == 2:
            arrived(kv_out.at[slot], from_2.at[0])
        else:
            for a in (0, 1):
                arrived(kv_out.at[slot, a], from_x.at[(4 - r) // 2, a, 0])
        push(kv_out.at[slot], kv_out.at[slot], from_pair.at[0, r], to_pair)
        if r == 2:
            arrived(oth.at[src, kv], from_2.at[1])
        else:
            for a in (0, 1):
                arrived(oth.at[src, a], from_x.at[(4 - r) // 2, a, 1])
        push(oth.at[src, kv], kv_out.at[slot], from_mirror.at[0, r], to_mirror)
        push(kv_out.at[slot], kv_out.at[slot], from_core.at[0, r], to_core)
    push(oth.at[x, qg], qg_out.at[4 + x], from_mirror.at[1, 0], to_mirror)
    for r in (0, 3, 1, 2):
        slot = index(mirror, x + r, c)
        arrived(kv_out.at[slot], from_mirror.at[0, r])
        push(kv_out.at[slot], kv_out.at[slot], from_pair.at[1, r], to_pair)
        push(kv_out.at[slot], kv_out.at[slot], from_core.at[1, r], to_core)
    relay((2, 3), 2)
    for r in (3, 1, 2):
        src = (x + r) % 4
        if r == 2:
            arrived(oth.at[src, qg], from_2.at[3])
        else:
            for a in (2, 3):
                arrived(oth.at[src, a], from_x.at[(4 - r) // 2, a, 1])
        push(oth.at[src, qg], qg_out.at[4 + src], from_mirror.at[1, r], to_mirror)
    rd_load.wait()
    for d in (1, 2, 3):
        arrived(rdx.at[(x + 4 - d) % 4], from_rd.at[d])
    push(rdx, rdm, from_rd.at[0], to_mirror)
    for m, zz in ((0, pair), (1, 3 - pair)):
        for r in (0, 3, 1, 2):
            slot = index(zz, x + r, c)
            arrived(kv_out.at[slot], from_pair.at[m, r])
            push(kv_out.at[slot], kv_out.at[slot], from_core.at[2 + m, r], to_core)
    for r in (3, 1, 2):
        src = (x + r) % 4
        if r == 2:
            arrived(qg_out.at[src], from_2.at[2])
        else:
            for a in (2, 3):
                arrived(qg_out.at[src, a - 2], from_x.at[(4 - r) // 2, a, 0])
    for r in range(4):
        arrived(qg_out.at[4 + (x + r) % 4], from_mirror.at[1, r])
        for m, zz in enumerate((z, mirror, pair, 3 - pair)):
            arrived(kv_out.at[index(zz, x + r, core)], from_core.at[m, r])
    arrived(rdm, from_rd.at[0])
    for copy in stores:
        copy.wait()
    for copy in sends:
        copy.wait_send()


def fetch(k, v, q, g, rd):
    anywhere = pl.BlockSpec(memory_space=pl.ANY)
    vmem = pl.BlockSpec(memory_space=pltpu.VMEM)
    dma = pltpu.SemaphoreType.DMA
    return pl.pallas_call(
        fetch_kernel,
        out_shape=(
            jax.ShapeDtypeStruct((32, 2, 512, DH), jnp.bfloat16),
            jax.ShapeDtypeStruct((8, 2, 512, DH), jnp.bfloat16),
            jax.ShapeDtypeStruct((4, 8, 128), jnp.float32),
            jax.ShapeDtypeStruct((4, 8, 128), jnp.float32),
        ),
        in_specs=[anywhere] * 5,
        out_specs=(anywhere, anywhere, vmem, vmem),
        scratch_shapes=[
            pltpu.VMEM((4, 512, DH), jnp.bfloat16),
            pltpu.VMEM((4, 4, 512, DH), jnp.bfloat16),
            pltpu.VMEM((2, 4, 512, DH), jnp.bfloat16),
            dma((80,)),
            dma((12,)),
            dma((2, 4, 2)),
            dma((4,)),
            dma((2, 4)),
            dma((2, 4)),
            dma((2, 4)),
            dma((4, 4)),
            dma((4,)),
        ],
        compiler_params=pltpu.CompilerParams(collective_id=0, has_side_effects=True),
    )(k, v, q, g, rd)


def attend_kernel(tab, edge, acc_tab, qg_ref, rd_ref, kv_ref, dq_ref, dkv_ref, acc_ref):
    acc_ref[...] = jnp.zeros_like(acc_ref)
    lane = lax.broadcasted_iota(jnp.int32, (1, 8 * BS), 1)
    eye = lax.broadcasted_iota(jnp.int32, (BS, BS), 0) == lax.broadcasted_iota(
        jnp.int32, (BS, BS), 1
    )

    def step(i, carry):
        slots = [tab[i * 8 + j] for j in range(8)]
        acc_slots = [acc_tab[i * 8 + j] for j in range(8)]
        at = i // 8 * 16 + i % 8
        keys = jnp.concatenate([kv_ref[p] for p in slots], axis=0)
        values = jnp.concatenate([kv_ref[p + 8] for p in slots], axis=0)
        q = qg_ref[at]
        g = qg_ref[at + 8]
        state = edge[i]
        gone = ((lane < BS) & (state == 1)) | (
            (lane >= 2 * BS) & (lane < 3 * BS) & (state == 2)
        )
        bias = jnp.where(gone, -jnp.inf, 0.0)
        scores = dot(q, keys, NT) * SCALE + bias
        peak = jnp.max(scores, axis=1, keepdims=True)
        e = jnp.exp(scores - peak)
        weights = e * (1.0 / jnp.sum(e, axis=1, keepdims=True))
        rd = jnp.sum(jnp.where(eye, rd_ref[pl.ds(i, 1), :], 0.0), axis=1, keepdims=True)
        ds = weights * (dot(g, values, NT) - rd)
        wb = weights.astype(jnp.bfloat16)
        dsb = ds.astype(jnp.bfloat16)
        dq_ref[i] = (dot(dsb, keys, (((1,), (0,)), ((), ()))) * SCALE).astype(jnp.bfloat16)
        dk = dot(dsb, q, TN) * SCALE
        dv = dot(wb, g, TN)
        for j, p in enumerate(acc_slots):
            acc_ref[p] += dk[j * BS : (j + 1) * BS]
            acc_ref[p + 8] += dv[j * BS : (j + 1) * BS]
        return carry

    lax.fori_loop(0, 64, step, 0)
    dkv_ref[...] = acc_ref[...].astype(jnp.bfloat16)


def attend(tab, edge, acc_tab, qg, rd, kv):
    vmem = pl.BlockSpec(memory_space=pltpu.VMEM)
    smem = pl.BlockSpec(memory_space=pltpu.SMEM)
    return pl.pallas_call(
        attend_kernel,
        out_shape=(
            jax.ShapeDtypeStruct((64, BS, DH), jnp.bfloat16),
            jax.ShapeDtypeStruct((512, BS, DH), jnp.bfloat16),
        ),
        in_specs=[smem, smem, smem, vmem, vmem, vmem],
        out_specs=(vmem, vmem),
        scratch_shapes=[pltpu.VMEM((512, BS, DH), jnp.float32)],
        compiler_params=pltpu.CompilerParams(vmem_limit_bytes=60 * 1024 * 1024),
    )(tab, edge, acc_tab, qg, rd, kv)


def place(block, zhi):
    z, x, c = block // 64, block // 16 % 4, block // 8 % 2
    near = z // 2 == zhi
    zlo = jnp.where(near, z % 2, (3 - z) % 2)
    slot = ((zlo * 2 + c) * 2 + jnp.where(near, 0, 1)) * 4 + x
    return slot * 16 + block % 8


def tables(random_blocks, global_blocks, z, x, c):
    zhi = z // 2
    mine = lax.dynamic_index_in_dim(random_blocks, x * 2 + zhi, 1, keepdims=False)
    mine = mine.reshape(4, 4, 2, 8, 3)
    mine = lax.dynamic_index_in_dim(mine, c, 2, keepdims=False)
    near = lax.dynamic_index_in_dim(mine, z, 0, keepdims=False)
    far = lax.dynamic_index_in_dim(mine, 3 - z, 0, keepdims=False)
    rand = jnp.stack([near, far]).reshape(64, 3)
    ids = jnp.arange(64, dtype=jnp.int32)
    zs = jnp.where(ids < 32, z, 3 - z)
    block = zs * 64 + ids // 8 % 4 * 16 + c * 8 + ids % 8
    window = jnp.stack([block - 1, block, block + 1], axis=1)
    window = jnp.clip(window, 0, 255)
    globs = jnp.broadcast_to(global_blocks[None], (64, 2))
    table = jnp.concatenate([window, rand, globs], axis=1)
    acc_table = place(table, zhi)
    table = table // 8 * 16 + table % 8
    edge = jnp.where(block == 0, 1, jnp.where(block == 255, 2, 0))
    return table.reshape(512), edge, acc_table.reshape(512)


def on_device(
    queries, key_states, value_states, forward_out, grad_out, random_blocks, global_blocks
):
    s = lax.axis_index("seq")
    z, x, c = s // 8, s // 2 % 4, s % 2
    zhi = z // 2
    tab, edge, acc_tab = tables(random_blocks, global_blocks, z, x, c)
    row_dot = jnp.sum(
        (grad_out.astype(jnp.float32) * forward_out.astype(jnp.float32)).reshape(512, 8, DH),
        axis=2,
    )

    def over_x(a):
        return lax.all_to_all(a, "seq", 0, 0, axis_index_groups=X_GROUPS, tiled=True)

    kv, qg, rdx, rdm = fetch(
        key_states, value_states, queries, grad_out, row_dot.T.reshape(4, 8, 128)
    )
    rd = lax.dynamic_index_in_dim(
        jnp.stack([rdx, rdm]).reshape(2, 4, 2, 512), zhi, 2, keepdims=False
    )
    dq, dkv = attend(
        tab,
        edge,
        acc_tab,
        qg.reshape(128, BS, DH),
        rd.reshape(64, BS),
        kv.reshape(512, BS, DH),
    )
    dkv = lax.psum_scatter(
        dkv.reshape(4, 2, 4, 2, 512, DH), "seq", axis_index_groups=HEAD_GROUPS
    )
    full = jnp.concatenate([dq.reshape(2, 4, 1, 512, DH), dkv], axis=2)
    near, far = full[0], lax.ppermute(full[1], "seq", MIRROR)
    low = zhi == 0
    both = jnp.stack([jnp.where(low, near, far), jnp.where(low, far, near)], axis=3)
    rows = over_x(both.reshape(4, 3, 512, 2 * DH)).transpose(1, 2, 0, 3).reshape(3, 512, 1024)
    outs = lax.all_to_all(rows, "head", split_axis=1, concat_axis=2, tiled=True)
    return outs[0], outs[1], outs[2]


def solution(mesh):
    return jax.shard_map(
        on_device,
        mesh=mesh,
        in_specs=(
            P("seq", "head"),
            P("seq", "head"),
            P("seq", "head"),
            P("seq", "head"),
            P("seq", "head"),
            P(None, "head", None),
            P(),
        ),
        out_specs=(P(("seq", "head"), None), P(("seq", "head"), None), P(("seq", "head"), None)),
        check_vma=False,
    )
```

```python
import jax
import jax.numpy as jnp
from jax import lax
from jax.experimental import pallas as pl
from jax.experimental.pallas import tpu as pltpu
from jax.sharding import PartitionSpec as P

DH = 128
BS = 64
SCALE = DH**-0.5
NT = (((1,), (1,)), ((), ()))
TN = (((0,), (0,)), ((), ()))


def dot(a, b, dims):
    return lax.dot_general(a, b, dims, preferred_element_type=jnp.float32)


MESH = pl.DeviceIdType.MESH


def index(z, x, c):
    return z * 8 + x % 4 * 2 + c


class Mover:
    def __init__(self, send, local):
        self.send, self.local = send, local
        self.sent, self.moved = [], []

    def push(self, src, dst, sem, peer):
        copy = pltpu.make_async_remote_copy(
            src_ref=src,
            dst_ref=dst,
            send_sem=self.send.at[len(self.sent)],
            recv_sem=sem,
            device_id=peer,
            device_id_type=MESH,
        )
        copy.start()
        self.sent.append(copy)

    def arrived(self, dst, sem, peer):
        pltpu.make_async_remote_copy(
            src_ref=dst,
            dst_ref=dst,
            send_sem=self.send.at[0],
            recv_sem=sem,
            device_id=peer,
            device_id_type=MESH,
        ).wait_recv()

    def move(self, src, dst):
        copy = pltpu.make_async_copy(src, dst, self.local.at[len(self.moved)])
        copy.start()
        self.moved.append(copy)
        return copy


def greet(peers):
    barrier = pltpu.get_barrier_semaphore()
    for peer in peers:
        pl.semaphore_signal(barrier, inc=1, device_id=peer, device_id_type=MESH)
    pl.semaphore_wait(barrier, len(peers))


def fetch_kernel(
    k_ref, v_ref, q_ref, g_ref, rd_ref,
    kv_out, qg_out, rdx, rdm,
    loc, oth,
    send, local, from_x, from_pair, from_mirror, from_core, from_rd,
):
    s = lax.axis_index("seq")
    z, x, c = s // 8, s // 2 % 4, s % 2
    zhi = z // 2
    mirror, pair, core = 3 - z, z + 1 - 2 * (z % 2), 1 - c
    to_mirror = {"seq": index(mirror, x, c)}
    to_pair = {"seq": index(pair, x, c)}
    to_core = {"seq": index(z, x, core)}
    along_x = [{"seq": index(z, x + d, c)} for d in range(4)]
    greet(along_x[1:] + [to_mirror, to_pair, to_core])
    mover = Mover(send, local)
    push, move = mover.push, mover.move

    def arrived(dst, sem):
        mover.arrived(dst, sem, to_core)

    ins = (k_ref, v_ref, q_ref, g_ref)
    kv = pl.ds(0, 2)
    qg = pl.ds(2, 2)

    def head(a, xx, half):
        return ins[a].at[:, pl.ds(pl.multiple_of(xx % 4 * 256 + half * DH, DH), DH)]

    def send_own(d, arrays):
        for a in arrays:
            dst = kv_out.at[s, a] if a < 2 else qg_out.at[x, a - 2]
            push(head(a, x + d, zhi), dst, from_x.at[d - 1, a, 0], along_x[d])

    def send_other(d, arrays):
        for a in arrays:
            push(head(a, x + d, 1 - zhi), oth.at[x, a], from_x.at[d - 1, a, 1], along_x[d])

    def slot_of(zz, r, cc=c):
        return kv_out.at[index(zz, x + r, cc)]

    def on_to_pair(m, r):
        slot = slot_of(mirror if m else z, r)
        push(slot, slot, from_pair.at[m, r], to_pair)
        push(slot, slot, from_core.at[m, r], to_core)

    def own_kv(r):
        for a in (0, 1):
            arrived(slot_of(z, r).at[a], from_x.at[3 - r, a, 0])
        on_to_pair(0, r)

    def other_kv(r):
        src = (x + r) % 4
        for a in (0, 1):
            arrived(oth.at[src, a], from_x.at[3 - r, a, 1])
        push(oth.at[src, kv], slot_of(z, r), from_mirror.at[0, r], to_mirror)

    def mirror_kv(r):
        arrived(slot_of(mirror, r), from_mirror.at[0, r])
        on_to_pair(1, r)

    def pair_kv(m, r):
        slot = slot_of(3 - pair if m else pair, r)
        arrived(slot, from_pair.at[m, r])
        push(slot, slot, from_core.at[2 + m, r], to_core)

    def other_qg(r):
        src = (x + r) % 4
        for a in (2, 3):
            arrived(oth.at[src, a], from_x.at[3 - r, a, 1])
        push(oth.at[src, qg], qg_out.at[4 + src], from_mirror.at[1, r], to_mirror)

    loads = [
        [move(head(a, x, zhi), loc.at[a]), move(head(a, x, 1 - zhi), oth.at[x, a])]
        for a in range(4)
    ]
    rd_load = move(rd_ref.at[x], rdx.at[x])
    send_own(1, (0, 1))
    send_own(3, (0, 1))
    send_other(1, (0, 1))
    send_other(3, (0, 1))
    for a in (0, 1):
        loads[a][0].wait()
        loads[a][1].wait()
    push(loc.at[kv], kv_out.at[s], from_pair.at[0, 0], to_pair)
    push(oth.at[x, kv], kv_out.at[s], from_mirror.at[0, 0], to_mirror)
    push(loc.at[kv], kv_out.at[s], from_core.at[0, 0], to_core)
    stores = [move(loc.at[kv], kv_out.at[s])]
    for d in (1, 2, 3):
        push(rd_ref.at[(x + d) % 4], rdx.at[x], from_rd.at[d], along_x[d])
    send_other(2, (0, 1))
    send_own(2, (0, 1))
    for d in (1, 3, 2):
        send_other(d, (2, 3))
    for d in (1, 3, 2):
        send_own(d, (2, 3))
    for a in (2, 3):
        loads[a][0].wait()
        loads[a][1].wait()
    push(oth.at[x, qg], qg_out.at[4 + x], from_mirror.at[1, 0], to_mirror)
    stores.append(move(loc.at[qg], qg_out.at[x]))
    mirror_kv(0)
    own_kv(3)
    own_kv(1)
    pair_kv(0, 0)
    other_kv(3)
    other_kv(1)
    rd_load.wait()
    for d in (1, 2, 3):
        arrived(rdx.at[(x + 4 - d) % 4], from_rd.at[d])
    push(rdx, rdm, from_rd.at[0], to_mirror)
    pair_kv(1, 0)
    mirror_kv(3)
    other_kv(2)
    mirror_kv(1)
    own_kv(2)
    pair_kv(0, 3)
    pair_kv(0, 1)
    other_qg(3)
    other_qg(1)
    mirror_kv(2)
    pair_kv(1, 3)
    other_qg(2)
    pair_kv(1, 1)
    pair_kv(0, 2)
    pair_kv(1, 2)
    for r in (3, 1, 2):
        for a in (2, 3):
            arrived(qg_out.at[(x + r) % 4, a - 2], from_x.at[3 - r, a, 0])
    for r in range(4):
        arrived(qg_out.at[4 + (x + r) % 4], from_mirror.at[1, r])
        for m, zz in enumerate((z, mirror, pair, 3 - pair)):
            arrived(slot_of(zz, r, core), from_core.at[m, r])
    arrived(rdm, from_rd.at[0])
    for copy in stores:
        copy.wait()
    for copy in mover.sent:
        copy.wait_send()


def fetch(k, v, q, g, rd):
    anywhere = pl.BlockSpec(memory_space=pl.ANY)
    vmem = pl.BlockSpec(memory_space=pltpu.VMEM)
    dma = pltpu.SemaphoreType.DMA
    return pl.pallas_call(
        fetch_kernel,
        out_shape=(
            jax.ShapeDtypeStruct((32, 2, 512, DH), jnp.bfloat16),
            jax.ShapeDtypeStruct((8, 2, 512, DH), jnp.bfloat16),
            jax.ShapeDtypeStruct((4, 8, 128), jnp.float32),
            jax.ShapeDtypeStruct((4, 8, 128), jnp.float32),
        ),
        in_specs=[anywhere] * 5,
        out_specs=(anywhere, anywhere, vmem, vmem),
        scratch_shapes=[
            pltpu.VMEM((4, 512, DH), jnp.bfloat16),
            pltpu.VMEM((4, 4, 512, DH), jnp.bfloat16),
            dma((64,)),
            dma((11,)),
            dma((3, 4, 2)),
            dma((2, 4)),
            dma((2, 4)),
            dma((4, 4)),
            dma((4,)),
        ],
        compiler_params=pltpu.CompilerParams(collective_id=0, has_side_effects=True),
    )(k, v, q, g, rd)


def give_kernel(
    dq_ref, dkv_ref, out_ref,
    part, near, far,
    send, local, from_core, from_pair, from_all,
):
    s = lax.axis_index("seq")
    y = lax.axis_index("head")
    z, x, c = s // 8, s // 2 % 4, s % 2
    zhi = z // 2
    mirror, pair, core = 3 - z, z + 1 - 2 * (z % 2), 1 - c
    to_pair = {"seq": index(pair, x, c), "head": y}
    to_core = {"seq": index(z, x, core), "head": y}
    order = (1, 3, 2, 0)

    def owner(m, r, t):
        return {"seq": index(mirror if m else z, x + r, c), "head": (y + t) % 4}

    peers = [
        owner(m, r, t) for m in (0, 1) for r in range(4) for t in range(4) if (m, r, t) != (0, 0, 0)
    ]
    greet([to_core, to_pair] + peers)
    mover = Mover(send, local)
    push, move = mover.push, mover.move
    classes = (3 - pair, pair, mirror, z)

    def spread(m, r, src, kind):
        col = pl.ds(pl.multiple_of(y * 1024 + (x * 2 + zhi) * DH, DH), DH)
        stores = []
        for t in order:
            rows = pl.ds(pl.multiple_of((y + t) % 4 * 128, 128), 128)
            if kind == 0:
                piece, dst = src.at[rows], out_ref.at[0, :, col]
            else:
                piece, dst = src.at[:, rows], out_ref.at[pl.ds(1, 2), :, col]
            if (m, r, t) == (0, 0, 0):
                stores.append(move(piece, dst))
            else:
                push(piece, dst, from_all.at[kind, m, r, t], owner(m, r, t))
        return stores

    loads = {}
    for cls in range(4):
        for r in range(4):
            at = index(classes[cls], x + r, c)
            loads[cls, r] = move(dkv_ref.at[at], part.at[cls, r])
            away = index(classes[cls], x + r, core)
            push(dkv_ref.at[away], near.at[cls, r], from_core.at[cls, r], to_core)
    kept = []
    for m in (1, 0):
        for r in order:
            kept += spread(m, r, dq_ref.at[m * 4 + (x + r) % 4], 0)

    def add(dst, terms):
        @pl.loop(0, 8)
        def _(i):
            rows = pl.ds(pl.multiple_of(i * 64, 64), 64)
            for a in range(2):
                total = terms[0][a, rows, :].astype(jnp.float32)
                for term in terms[1:]:
                    total += term[a, rows, :].astype(jnp.float32)
                dst[a, rows, :] = total.astype(jnp.bfloat16)

    for cls in (0, 1):
        for r in order:
            loads[cls, r].wait()
            mover.arrived(near.at[cls, r], from_core.at[cls, r], to_core)
            mine = part.at[cls, r]
            add(mine, (mine, near.at[cls, r]))
            push(mine, far.at[cls, r], from_pair.at[cls, r], to_pair)
    for cls in (2, 3):
        for r in order:
            loads[cls, r].wait()
            mover.arrived(near.at[cls, r], from_core.at[cls, r], to_core)
            mover.arrived(far.at[cls - 2, r], from_pair.at[cls - 2, r], to_pair)
            mine = part.at[cls, r]
            add(mine, (mine, near.at[cls, r], far.at[cls - 2, r]))
            kept += spread(3 - cls, r, mine, 1)
    for m in (0, 1):
        for r in range(4):
            for t in range(4):
                if (m, r, t) == (0, 0, 0):
                    continue
                half = 1 - zhi if m else zhi
                from_head = (x + 4 - r) % 4 * 2 + half
                col = pl.multiple_of((y + 4 - t) % 4 * 1024 + from_head * DH, DH)
                for kind in (0, 1):
                    piece = (
                        out_ref.at[0, :, pl.ds(col, DH)]
                        if kind == 0
                        else out_ref.at[pl.ds(1, 2), :, pl.ds(col, DH)]
                    )
                    mover.arrived(piece, from_all.at[kind, m, r, t], to_core)
    for copy in kept:
        copy.wait()
    for copy in mover.sent:
        copy.wait_send()


def give(dq, dkv):
    anywhere = pl.BlockSpec(memory_space=pl.ANY)
    dma = pltpu.SemaphoreType.DMA
    return pl.pallas_call(
        give_kernel,
        out_shape=jax.ShapeDtypeStruct((3, 128, 4096), jnp.bfloat16),
        in_specs=[anywhere] * 2,
        out_specs=anywhere,
        scratch_shapes=[
            pltpu.VMEM((4, 4, 2, 512, DH), jnp.bfloat16),
            pltpu.VMEM((4, 4, 2, 512, DH), jnp.bfloat16),
            pltpu.VMEM((2, 4, 2, 512, DH), jnp.bfloat16),
            dma((86,)),
            dma((18,)),
            dma((4, 4)),
            dma((2, 4)),
            dma((2, 2, 4, 4)),
        ],
        compiler_params=pltpu.CompilerParams(collective_id=1, has_side_effects=True),
    )(dq, dkv)


def attend_kernel(tab, edge, qg_ref, rd_ref, kv_ref, dq_ref, dkv_ref, acc_ref):
    acc_ref[...] = jnp.zeros_like(acc_ref)
    lane = lax.broadcasted_iota(jnp.int32, (1, 8 * BS), 1)
    eye = lax.broadcasted_iota(jnp.int32, (BS, BS), 0) == lax.broadcasted_iota(
        jnp.int32, (BS, BS), 1
    )

    def step(i, carry):
        slots = [tab[i * 8 + j] for j in range(8)]
        at = i // 8 * 16 + i % 8
        keys = jnp.concatenate([kv_ref[p] for p in slots], axis=0)
        values = jnp.concatenate([kv_ref[p + 8] for p in slots], axis=0)
        q = qg_ref[at]
        g = qg_ref[at + 8]
        state = edge[i]
        gone = ((lane < BS) & (state == 1)) | (
            (lane >= 2 * BS) & (lane < 3 * BS) & (state == 2)
        )
        bias = jnp.where(gone, -jnp.inf, 0.0)
        scores = dot(q, keys, NT) * SCALE + bias
        peak = jnp.max(scores, axis=1, keepdims=True)
        e = jnp.exp(scores - peak)
        weights = e * (1.0 / jnp.sum(e, axis=1, keepdims=True))
        rd = jnp.sum(jnp.where(eye, rd_ref[pl.ds(i, 1), :], 0.0), axis=1, keepdims=True)
        ds = weights * (dot(g, values, NT) - rd)
        wb = weights.astype(jnp.bfloat16)
        dsb = ds.astype(jnp.bfloat16)
        dq_ref[i] = (dot(dsb, keys, (((1,), (0,)), ((), ()))) * SCALE).astype(jnp.bfloat16)
        dk = dot(dsb, q, TN) * SCALE
        dv = dot(wb, g, TN)
        for j, p in enumerate(slots):
            acc_ref[p] += dk[j * BS : (j + 1) * BS]
            acc_ref[p + 8] += dv[j * BS : (j + 1) * BS]
        return carry

    lax.fori_loop(0, 64, step, 0)
    dkv_ref[...] = acc_ref[...].astype(jnp.bfloat16)


def attend(tab, edge, qg, rd, kv):
    vmem = pl.BlockSpec(memory_space=pltpu.VMEM)
    smem = pl.BlockSpec(memory_space=pltpu.SMEM)
    return pl.pallas_call(
        attend_kernel,
        out_shape=(
            jax.ShapeDtypeStruct((64, BS, DH), jnp.bfloat16),
            jax.ShapeDtypeStruct((512, BS, DH), jnp.bfloat16),
        ),
        in_specs=[smem, smem, vmem, vmem, vmem],
        out_specs=(vmem, vmem),
        scratch_shapes=[pltpu.VMEM((512, BS, DH), jnp.float32)],
        compiler_params=pltpu.CompilerParams(vmem_limit_bytes=60 * 1024 * 1024),
    )(tab, edge, qg, rd, kv)


def tables(random_blocks, global_blocks, z, x, c):
    zhi = z // 2
    mine = lax.dynamic_index_in_dim(random_blocks, x * 2 + zhi, 1, keepdims=False)
    mine = mine.reshape(4, 4, 2, 8, 3)
    mine = lax.dynamic_index_in_dim(mine, c, 2, keepdims=False)
    near = lax.dynamic_index_in_dim(mine, z, 0, keepdims=False)
    far = lax.dynamic_index_in_dim(mine, 3 - z, 0, keepdims=False)
    rand = jnp.stack([near, far]).reshape(64, 3)
    ids = jnp.arange(64, dtype=jnp.int32)
    zs = jnp.where(ids < 32, z, 3 - z)
    block = zs * 64 + ids // 8 % 4 * 16 + c * 8 + ids % 8
    window = jnp.stack([block - 1, block, block + 1], axis=1)
    window = jnp.clip(window, 0, 255)
    globs = jnp.broadcast_to(global_blocks[None], (64, 2))
    table = jnp.concatenate([window, rand, globs], axis=1)
    table = table // 8 * 16 + table % 8
    edge = jnp.where(block == 0, 1, jnp.where(block == 255, 2, 0))
    return table.reshape(512), edge


def on_device(
    queries, key_states, value_states, forward_out, grad_out, random_blocks, global_blocks
):
    s = lax.axis_index("seq")
    z, x, c = s // 8, s // 2 % 4, s % 2
    zhi = z // 2
    tab, edge = tables(random_blocks, global_blocks, z, x, c)
    row_dot = jnp.sum(
        (grad_out.astype(jnp.float32) * forward_out.astype(jnp.float32)).reshape(512, 8, DH),
        axis=2,
    )

    kv, qg, rdx, rdm = fetch(
        key_states, value_states, queries, grad_out, row_dot.T.reshape(4, 8, 128)
    )
    rd = lax.dynamic_index_in_dim(
        jnp.stack([rdx, rdm]).reshape(2, 4, 2, 512), zhi, 2, keepdims=False
    )
    dq, dkv = attend(
        tab,
        edge,
        qg.reshape(128, BS, DH),
        rd.reshape(64, BS),
        kv.reshape(512, BS, DH),
    )
    outs = give(dq.reshape(8, 512, DH), dkv.reshape(32, 2, 512, DH))
    return outs[0], outs[1], outs[2]


def solution(mesh):
    return jax.shard_map(
        on_device,
        mesh=mesh,
        in_specs=(
            P("seq", "head"),
            P("seq", "head"),
            P("seq", "head"),
            P("seq", "head"),
            P("seq", "head"),
            P(None, "head", None),
            P(),
        ),
        out_specs=(P(("seq", "head"), None), P(("seq", "head"), None), P(("seq", "head"), None)),
        check_vma=False,
    )
```

```python
import jax
import jax.numpy as jnp
from jax import lax
from jax.experimental import pallas as pl
from jax.experimental.pallas import tpu as pltpu
from jax.sharding import PartitionSpec as P

DH = 128
BS = 64
SCALE = DH**-0.5
SCALE_LOG2E = SCALE * 1.4426950408889634
ATTEND_VMEM = 60 * 1024 * 1024
NT = (((1,), (1,)), ((), ()))
TN = (((0,), (0,)), ((), ()))
NN = (((1,), (0,)), ((), ()))


def dot(a, b, dims):
    return lax.dot_general(a, b, dims, preferred_element_type=jnp.float32)


MESH = pl.DeviceIdType.MESH


def index(z, x, c):
    return z * 8 + x % 4 * 2 + c


class Mover:
    def __init__(self, send, local):
        self.send, self.local = send, local
        self.sent, self.moved = [], []

    def push(self, src, dst, sem, peer):
        copy = pltpu.make_async_remote_copy(
            src_ref=src,
            dst_ref=dst,
            send_sem=self.send.at[len(self.sent)],
            recv_sem=sem,
            device_id=peer,
            device_id_type=MESH,
        )
        copy.start()
        self.sent.append(copy)

    def arrived(self, dst, sem, peer):
        pltpu.make_async_remote_copy(
            src_ref=dst,
            dst_ref=dst,
            send_sem=self.send.at[0],
            recv_sem=sem,
            device_id=peer,
            device_id_type=MESH,
        ).wait_recv()

    def move(self, src, dst):
        copy = pltpu.make_async_copy(src, dst, self.local.at[len(self.moved)])
        copy.start()
        self.moved.append(copy)
        return copy


def greet(peers):
    barrier = pltpu.get_barrier_semaphore()
    for peer in peers:
        pl.semaphore_signal(barrier, inc=1, device_id=peer, device_id_type=MESH)
    pl.semaphore_wait(barrier, len(peers))


def fetch_kernel(
    k_ref, v_ref, q_ref, g_ref, o_ref,
    kv_out, qg_out, rd_out,
    loc, oth, rd_mine, g_all, o_all,
    send, local, from_x, from_pair, from_mirror, from_core, from_rd,
):
    s = lax.axis_index("seq")
    z, x, c = s // 8, s // 2 % 4, s % 2
    zhi = z // 2
    mirror, pair, core = 3 - z, z + 1 - 2 * (z % 2), 1 - c
    to_mirror = {"seq": index(mirror, x, c)}
    to_pair = {"seq": index(pair, x, c)}
    to_core = {"seq": index(z, x, core)}
    along_x = [{"seq": index(z, x + d, c)} for d in range(4)]
    greet(along_x[1:] + [to_mirror, to_pair, to_core])
    mover = Mover(send, local)
    push, move = mover.push, mover.move

    def arrived(dst, sem):
        mover.arrived(dst, sem, to_core)

    ins = (k_ref, v_ref, q_ref, g_ref)
    kv = pl.ds(0, 2)
    qg = pl.ds(2, 2)

    def head(a, xx, half):
        return ins[a].at[:, pl.ds(pl.multiple_of(xx % 4 * 256 + half * DH, DH), DH)]

    def send_own(d, arrays):
        for a in arrays:
            dst = kv_out.at[s, a] if a < 2 else qg_out.at[x, a - 2]
            push(head(a, x + d, zhi), dst, from_x.at[d - 1, a, 0], along_x[d])

    def send_other(d, arrays):
        for a in arrays:
            push(head(a, x + d, 1 - zhi), oth.at[x, a], from_x.at[d - 1, a, 1], along_x[d])

    def slot_of(zz, r, cc=c):
        return kv_out.at[index(zz, x + r, cc)]

    def on_to_pair(m, r):
        slot = slot_of(mirror if m else z, r)
        push(slot, slot, from_pair.at[m, r], to_pair)
        push(slot, slot, from_core.at[m, r], to_core)

    def own_kv(r):
        for a in (0, 1):
            arrived(slot_of(z, r).at[a], from_x.at[3 - r, a, 0])
        on_to_pair(0, r)

    def other_kv(r):
        src = (x + r) % 4
        for a in (0, 1):
            arrived(oth.at[src, a], from_x.at[3 - r, a, 1])
        push(oth.at[src, kv], slot_of(z, r), from_mirror.at[0, r], to_mirror)

    def mirror_kv(r):
        arrived(slot_of(mirror, r), from_mirror.at[0, r])
        on_to_pair(1, r)

    def pair_kv(m, r):
        slot = slot_of(3 - pair if m else pair, r)
        arrived(slot, from_pair.at[m, r])
        push(slot, slot, from_core.at[2 + m, r], to_core)

    def other_qg(r):
        src = (x + r) % 4
        for a in (2, 3):
            arrived(oth.at[src, a], from_x.at[3 - r, a, 1])
        push(oth.at[src, qg], qg_out.at[4 + src], from_mirror.at[1, r], to_mirror)

    loads = [
        [move(head(a, x, zhi), loc.at[a]), move(head(a, x, 1 - zhi), oth.at[x, a])]
        for a in range(4)
    ]
    dots = [move(g_ref, g_all), move(o_ref, o_all)]
    send_own(1, (0, 1))
    send_own(3, (0, 1))
    send_other(1, (0, 1))
    send_other(3, (0, 1))
    for a in (0, 1):
        loads[a][0].wait()
        loads[a][1].wait()
    push(loc.at[kv], kv_out.at[s], from_pair.at[0, 0], to_pair)
    push(oth.at[x, kv], kv_out.at[s], from_mirror.at[0, 0], to_mirror)
    push(loc.at[kv], kv_out.at[s], from_core.at[0, 0], to_core)
    stores = [move(loc.at[kv], kv_out.at[s])]
    send_other(2, (0, 1))
    send_own(2, (0, 1))
    for d in (1, 3, 2):
        send_other(d, (2, 3))
    for d in (1, 3, 2):
        send_own(d, (2, 3))
    for a in (2, 3):
        loads[a][0].wait()
        loads[a][1].wait()
    push(oth.at[x, qg], qg_out.at[4 + x], from_mirror.at[1, 0], to_mirror)
    stores.append(move(loc.at[qg], qg_out.at[x]))
    for load in dots:
        load.wait()

    @pl.loop(0, 4)
    def _(i):
        rows = pl.ds(pl.multiple_of(i * 128, 128), 128)
        for h in range(8):
            cols = slice(h * DH, (h + 1) * DH)
            terms = g_all[rows, cols].astype(jnp.float32) * o_all[rows, cols].astype(jnp.float32)
            rd_mine[h // 2, pl.ds(h % 2 * 4 + i, 1), :] = jnp.sum(terms.T, axis=0, keepdims=True)

    mirror_kv(0)
    own_kv(3)
    own_kv(1)
    pair_kv(0, 0)
    rd_load = move(rd_mine.at[x], rd_out.at[x])
    for d in (1, 2, 3):
        push(rd_mine.at[(x + d) % 4], rd_out.at[x], from_rd.at[d], along_x[d])
    other_kv(3)
    other_kv(1)
    pair_kv(1, 0)
    mirror_kv(3)
    other_kv(2)
    mirror_kv(1)
    own_kv(2)
    rd_load.wait()
    for d in (1, 2, 3):
        arrived(rd_out.at[(x + 4 - d) % 4], from_rd.at[d])
    near, far = pl.ds(0, 4), pl.ds(4, 4)
    push(rd_out.at[near], rd_out.at[far], from_rd.at[0], to_mirror)
    pair_kv(0, 3)
    pair_kv(0, 1)
    other_qg(3)
    other_qg(1)
    mirror_kv(2)
    pair_kv(1, 3)
    other_qg(2)
    pair_kv(1, 1)
    pair_kv(0, 2)
    pair_kv(1, 2)
    for r in (3, 1, 2):
        for a in (2, 3):
            arrived(qg_out.at[(x + r) % 4, a - 2], from_x.at[3 - r, a, 0])
    for r in range(4):
        arrived(qg_out.at[4 + (x + r) % 4], from_mirror.at[1, r])
        for m, zz in enumerate((z, mirror, pair, 3 - pair)):
            arrived(slot_of(zz, r, core), from_core.at[m, r])
    arrived(rd_out.at[far], from_rd.at[0])
    for copy in stores:
        copy.wait()
    for copy in mover.sent:
        copy.wait_send()


def fetch(k, v, q, g, o):
    anywhere = pl.BlockSpec(memory_space=pl.ANY)
    vmem = pl.BlockSpec(memory_space=pltpu.VMEM)
    dma = pltpu.SemaphoreType.DMA
    return pl.pallas_call(
        fetch_kernel,
        out_shape=(
            jax.ShapeDtypeStruct((32, 2, 512, DH), jnp.bfloat16),
            jax.ShapeDtypeStruct((8, 2, 512, DH), jnp.bfloat16),
            jax.ShapeDtypeStruct((8, 8, 128), jnp.float32),
        ),
        in_specs=[anywhere] * 5,
        out_specs=(anywhere, anywhere, vmem),
        scratch_shapes=[
            pltpu.VMEM((4, 512, DH), jnp.bfloat16),
            pltpu.VMEM((4, 4, 512, DH), jnp.bfloat16),
            pltpu.VMEM((4, 8, 128), jnp.float32),
            pltpu.VMEM((512, 1024), jnp.bfloat16),
            pltpu.VMEM((512, 1024), jnp.bfloat16),
            dma((64,)),
            dma((13,)),
            dma((3, 4, 2)),
            dma((2, 4)),
            dma((2, 4)),
            dma((4, 4)),
            dma((4,)),
        ],
        compiler_params=pltpu.CompilerParams(collective_id=0, has_side_effects=True),
    )(k, v, q, g, o)


def give_kernel(
    dq_ref, dkv_ref, out_ref,
    part, near, far,
    send, local, from_core, from_pair, from_all,
):
    s = lax.axis_index("seq")
    y = lax.axis_index("head")
    z, x, c = s // 8, s // 2 % 4, s % 2
    zhi = z // 2
    mirror, pair, core = 3 - z, z + 1 - 2 * (z % 2), 1 - c
    to_pair = {"seq": index(pair, x, c), "head": y}
    to_core = {"seq": index(z, x, core), "head": y}
    order = (1, 3, 2, 0)

    def owner(m, r, t):
        return {"seq": index(mirror if m else z, x + r, c), "head": (y + t) % 4}

    peers = [
        owner(m, r, t) for m in (0, 1) for r in range(4) for t in range(4) if (m, r, t) != (0, 0, 0)
    ]
    greet([to_core, to_pair] + peers)
    mover = Mover(send, local)
    push, move = mover.push, mover.move
    classes = (3 - pair, pair, mirror, z)

    def spread(m, r, src, kind):
        col = pl.ds(pl.multiple_of(y * 1024 + (x * 2 + zhi) * DH, DH), DH)
        stores = []
        for t in order:
            rows = pl.ds(pl.multiple_of((y + t) % 4 * 128, 128), 128)
            if kind == 0:
                piece, dst = src.at[rows], out_ref.at[0, :, col]
            else:
                piece, dst = src.at[:, rows], out_ref.at[pl.ds(1, 2), :, col]
            if (m, r, t) == (0, 0, 0):
                stores.append(move(piece, dst))
            else:
                push(piece, dst, from_all.at[kind, m, r, t], owner(m, r, t))
        return stores

    loads = {}
    for cls in range(4):
        for r in order:
            at = index(classes[cls], x + r, c)
            loads[cls, r] = move(dkv_ref.at[at], part.at[cls, r])
            away = index(classes[cls], x + r, core)
            push(dkv_ref.at[away], near.at[cls, r], from_core.at[cls, r], to_core)
    kept = []
    for m in (1, 0):
        for r in order:
            kept += spread(m, r, dq_ref.at[m * 4 + (x + r) % 4], 0)

    def add(dst, terms):
        @pl.loop(0, 8)
        def _(i):
            rows = pl.ds(pl.multiple_of(i * 64, 64), 64)
            for a in range(2):
                total = terms[0][a, rows, :].astype(jnp.float32)
                for term in terms[1:]:
                    total += term[a, rows, :].astype(jnp.float32)
                dst[a, rows, :] = total.astype(jnp.bfloat16)

    for cls in (0, 1):
        for r in order:
            loads[cls, r].wait()
            mover.arrived(near.at[cls, r], from_core.at[cls, r], to_core)
            mine = part.at[cls, r]
            add(mine, (mine, near.at[cls, r]))
            push(mine, far.at[cls, r], from_pair.at[cls, r], to_pair)
    for cls in (2, 3):
        for r in order:
            loads[cls, r].wait()
            mover.arrived(near.at[cls, r], from_core.at[cls, r], to_core)
            mover.arrived(far.at[cls - 2, r], from_pair.at[cls - 2, r], to_pair)
            mine = part.at[cls, r]
            add(mine, (mine, near.at[cls, r], far.at[cls - 2, r]))
            kept += spread(3 - cls, r, mine, 1)
    for m in (0, 1):
        for r in range(4):
            for t in range(4):
                if (m, r, t) == (0, 0, 0):
                    continue
                half = 1 - zhi if m else zhi
                from_head = (x + 4 - r) % 4 * 2 + half
                col = pl.multiple_of((y + 4 - t) % 4 * 1024 + from_head * DH, DH)
                for kind in (0, 1):
                    piece = (
                        out_ref.at[0, :, pl.ds(col, DH)]
                        if kind == 0
                        else out_ref.at[pl.ds(1, 2), :, pl.ds(col, DH)]
                    )
                    mover.arrived(piece, from_all.at[kind, m, r, t], to_core)
    for copy in kept:
        copy.wait()
    for copy in mover.sent:
        copy.wait_send()


def give(dq, dkv):
    anywhere = pl.BlockSpec(memory_space=pl.ANY)
    dma = pltpu.SemaphoreType.DMA
    return pl.pallas_call(
        give_kernel,
        out_shape=jax.ShapeDtypeStruct((3, 128, 4096), jnp.bfloat16),
        in_specs=[anywhere] * 2,
        out_specs=anywhere,
        scratch_shapes=[
            pltpu.VMEM((4, 4, 2, 512, DH), jnp.bfloat16),
            pltpu.VMEM((4, 4, 2, 512, DH), jnp.bfloat16),
            pltpu.VMEM((2, 4, 2, 512, DH), jnp.bfloat16),
            dma((86,)),
            dma((18,)),
            dma((4, 4)),
            dma((2, 4)),
            dma((2, 2, 4, 4)),
        ],
        compiler_params=pltpu.CompilerParams(collective_id=1, has_side_effects=True),
    )(dq, dkv)


def attend_kernel(
    tab, edge, qg_hbm, rd_ref, kv_hbm, dq_ref, dkv_hbm,
    qg_ref, kv_ref, acc_ref, s0, s1, w0, w1, d0, d1, p0, p1, arrive, leave,
):
    loads = [
        pltpu.make_async_copy(
            kv_hbm.at[pl.ds(i * 128, 128)], kv_ref.at[pl.ds(i * 128, 128)], arrive.at[i]
        )
        for i in range(4)
    ]
    loads.append(pltpu.make_async_copy(qg_hbm, qg_ref, arrive.at[4]))
    for load in loads:
        load.start()

    @pl.loop(0, 32)
    def _(i):
        acc_ref[pl.ds(i * 16, 16)] = jnp.zeros((16, BS, DH), jnp.float32)

    for load in loads:
        load.wait()
    first = lax.broadcasted_iota(jnp.int32, (1, 2 * BS), 1) < BS
    half = edge[64] * 4

    def slots_of(p):
        return [tab[p * 16 + j] for j in range(16)]

    def base_of(p):
        return p // 4 * 16 + p % 4 * 2

    def pair_rows(base):
        a, b = qg_ref[base], qg_ref[base + 1]
        zero = jnp.zeros_like(a)
        return jnp.concatenate(
            [jnp.concatenate([a, zero], axis=1), jnp.concatenate([zero, b], axis=1)], axis=0
        )

    def pair_keys(slots, offset):
        return jnp.concatenate(
            [
                jnp.concatenate([kv_ref[slots[j] + offset], kv_ref[slots[8 + j] + offset]], axis=1)
                for j in range(8)
            ],
            axis=0,
        )

    def score(p, s_ref, w_ref):
        slots, base = slots_of(p), base_of(p)
        s_ref[...] = dot(pair_keys(slots, 0), pair_rows(base), NT)
        w_ref[...] = dot(pair_keys(slots, 8), pair_rows(base + 8), NT)

    def soften(p, s_ref, w_ref, d_ref, p_ref):
        state = jnp.where(first, edge[2 * p], edge[2 * p + 1])
        low = jnp.where(state == 1, -jnp.inf, 0.0)
        high = jnp.where(state == 2, -jnp.inf, 0.0)
        s = s_ref[...] * SCALE_LOG2E
        s = jnp.concatenate(
            [s[:BS] + low, s[BS : 2 * BS], s[2 * BS : 3 * BS] + high, s[3 * BS :]], axis=0
        )
        e = jnp.exp2(s - jnp.max(s, axis=0, keepdims=True))
        weights = e * (1.0 / jnp.sum(e, axis=0, keepdims=True))
        p_ref[...] = weights.astype(jnp.bfloat16)
        rd = rd_ref[p // 4, pl.ds(half + p % 4, 1), :]
        d_ref[...] = (weights * (w_ref[...] - rd)).astype(jnp.bfloat16)

    def spread(p, d_ref, p_ref):
        slots, base = slots_of(p), base_of(p)
        d = d_ref[...]
        dq = dot(d, pair_keys(slots, 0), TN) * SCALE
        dq_ref[2 * p] = dq[:BS, :DH].astype(jnp.bfloat16)
        dq_ref[2 * p + 1] = dq[BS:, DH:].astype(jnp.bfloat16)
        dk = dot(d, pair_rows(base), NN)
        dv = dot(p_ref[...], pair_rows(base + 8), NN)
        for j in range(16):
            side, row = j // 8 * DH, j % 8 * BS
            acc_ref[slots[j]] += dk[row : row + BS, side : side + DH]
            acc_ref[slots[j] + 8] += dv[row : row + BS, side : side + DH]

    score(0, s0, w0)
    soften(0, s0, w0, d0, p0)
    score(1, s1, w1)

    @pl.loop(1, 16)
    def _(t):
        a = 2 * t
        spread(a - 2, d0, p0)
        soften(a - 1, s1, w1, d1, p1)
        score(a, s0, w0)
        spread(a - 1, d1, p1)
        soften(a, s0, w0, d0, p0)
        score(a + 1, s1, w1)

    soften(31, s1, w1, d1, p1)
    spread(30, d0, p0)
    spread(31, d1, p1)
    stores = []
    for i in range(8):

        @pl.loop(0, 4)
        def _(t):
            slot = pl.multiple_of(i * 64 + t * 16, 16)
            kv_ref[pl.ds(slot, 8)] = (acc_ref[pl.ds(slot, 8)] * SCALE).astype(jnp.bfloat16)
            kv_ref[pl.ds(slot + 8, 8)] = acc_ref[pl.ds(slot + 8, 8)].astype(jnp.bfloat16)

        part = pl.ds(i * 64, 64)
        stores.append(pltpu.make_async_copy(kv_ref.at[part], dkv_hbm.at[part], leave.at[i]))
        stores[-1].start()
    for store in stores:
        store.wait()


def attend(tab, edge, qg, rd, kv):
    vmem = pl.BlockSpec(memory_space=pltpu.VMEM)
    smem = pl.BlockSpec(memory_space=pltpu.SMEM)
    anywhere = pl.BlockSpec(memory_space=pl.ANY)
    return pl.pallas_call(
        attend_kernel,
        out_shape=(
            jax.ShapeDtypeStruct((64, BS, DH), jnp.bfloat16),
            jax.ShapeDtypeStruct((512, BS, DH), jnp.bfloat16),
        ),
        in_specs=[smem, smem, anywhere, vmem, anywhere],
        out_specs=(vmem, anywhere),
        scratch_shapes=[
            pltpu.VMEM((128, BS, DH), jnp.bfloat16),
            pltpu.VMEM((512, BS, DH), jnp.bfloat16),
            pltpu.VMEM((512, BS, DH), jnp.float32),
        ]
        + [pltpu.VMEM((8 * BS, 2 * BS), jnp.float32)] * 4
        + [pltpu.VMEM((8 * BS, 2 * BS), jnp.bfloat16)] * 4
        + [pltpu.SemaphoreType.DMA((5,)), pltpu.SemaphoreType.DMA((8,))],
        compiler_params=pltpu.CompilerParams(vmem_limit_bytes=ATTEND_VMEM),
    )(tab, edge, qg, rd, kv)


def tables(random_blocks, global_blocks, z, x, c):
    zhi = z // 2
    mine = lax.dynamic_index_in_dim(random_blocks, x * 2 + zhi, 1, keepdims=False)
    mine = mine.reshape(4, 4, 2, 8, 3)
    mine = lax.dynamic_index_in_dim(mine, c, 2, keepdims=False)
    near = lax.dynamic_index_in_dim(mine, z, 0, keepdims=False)
    far = lax.dynamic_index_in_dim(mine, 3 - z, 0, keepdims=False)
    rand = jnp.stack([near, far]).reshape(64, 3)
    ids = jnp.arange(64, dtype=jnp.int32)
    zs = jnp.where(ids < 32, z, 3 - z)
    block = zs * 64 + ids // 8 % 4 * 16 + c * 8 + ids % 8
    window = jnp.stack([block - 1, block, block + 1], axis=1)
    window = jnp.clip(window, 0, 255)
    globs = jnp.broadcast_to(global_blocks[None], (64, 2))
    table = jnp.concatenate([window, rand, globs], axis=1)
    table = table // 8 * 16 + table % 8
    edge = jnp.where(block == 0, 1, jnp.where(block == 255, 2, 0))
    edge = jnp.concatenate([edge, zhi[None].astype(edge.dtype)])
    return table.reshape(512), edge


def on_device(
    queries, key_states, value_states, forward_out, grad_out, random_blocks, global_blocks
):
    s = lax.axis_index("seq")
    z, x, c = s // 8, s // 2 % 4, s % 2
    zhi = z // 2
    tab, edge = tables(random_blocks, global_blocks, z, x, c)
    kv, qg, rd = fetch(key_states, value_states, queries, grad_out, forward_out)
    dq, dkv = attend(
        tab,
        edge,
        qg.reshape(128, BS, DH),
        rd,
        kv.reshape(512, BS, DH),
    )
    outs = give(dq.reshape(8, 512, DH), dkv.reshape(32, 2, 512, DH))
    return outs[0], outs[1], outs[2]


def solution(mesh):
    return jax.shard_map(
        on_device,
        mesh=mesh,
        in_specs=(
            P("seq", "head"),
            P("seq", "head"),
            P("seq", "head"),
            P("seq", "head"),
            P("seq", "head"),
            P(None, "head", None),
            P(),
        ),
        out_specs=(P(("seq", "head"), None), P(("seq", "head"), None), P(("seq", "head"), None)),
        check_vma=False,
    )
```

```python
import jax
import jax.numpy as jnp
from jax import lax
from jax.experimental import pallas as pl
from jax.experimental.pallas import tpu as pltpu
from jax.sharding import PartitionSpec as P

DH = 128
BS = 64
SCALE = DH**-0.5
SCALE_LOG2E = SCALE * 1.4426950408889634
ATTEND_VMEM = 24 * 1024 * 1024
FETCH_VMEM = 10 * 1024 * 1024
GIVE_VMEM = 16 * 1024 * 1024
NT = (((1,), (1,)), ((), ()))
TN = (((0,), (0,)), ((), ()))
NN = (((1,), (0,)), ((), ()))


def dot(a, b, dims):
    return lax.dot_general(a, b, dims, preferred_element_type=jnp.float32)


MESH = pl.DeviceIdType.MESH


def index(z, x, c):
    return z * 8 + x % 4 * 2 + c


class Mover:
    def __init__(self, send, local):
        self.send, self.local = send, local
        self.sent, self.moved = [], []

    def push(self, src, dst, sem, peer):
        copy = pltpu.make_async_remote_copy(
            src_ref=src,
            dst_ref=dst,
            send_sem=self.send.at[len(self.sent)],
            recv_sem=sem,
            device_id=peer,
            device_id_type=MESH,
        )
        copy.start()
        self.sent.append(copy)

    def arrived(self, dst, sem, peer):
        pltpu.make_async_remote_copy(
            src_ref=dst,
            dst_ref=dst,
            send_sem=self.send.at[0],
            recv_sem=sem,
            device_id=peer,
            device_id_type=MESH,
        ).wait_recv()

    def move(self, src, dst):
        copy = pltpu.make_async_copy(src, dst, self.local.at[len(self.moved)])
        copy.start()
        self.moved.append(copy)
        return copy


def greet(peers):
    barrier = pltpu.get_barrier_semaphore()
    for peer in peers:
        pl.semaphore_signal(barrier, inc=1, device_id=peer, device_id_type=MESH)
    pl.semaphore_wait(barrier, len(peers))


def fetch_kernel(
    k_ref, v_ref, q_ref, g_ref, o_ref,
    kv_out, qg_out, rd_out,
    oth, rd_mine, g_all, o_all,
    send, local, from_x, from_pair, from_mirror, from_core, from_rd,
):
    s = lax.axis_index("seq")
    z, x, c = s // 8, s // 2 % 4, s % 2
    zhi = z // 2
    mirror, pair, core = 3 - z, z + 1 - 2 * (z % 2), 1 - c
    to_mirror = {"seq": index(mirror, x, c)}
    to_pair = {"seq": index(pair, x, c)}
    to_core = {"seq": index(z, x, core)}
    along_x = [{"seq": index(z, x + d, c)} for d in range(4)]
    mover = Mover(send, local)
    push, move = mover.push, mover.move

    def arrived(dst, sem):
        mover.arrived(dst, sem, to_core)

    ins = (k_ref, v_ref, q_ref, g_ref)

    def head(a, xx, half):
        return ins[a].at[:, pl.ds(pl.multiple_of(xx % 4 * 256 + half * DH, DH), DH)]

    def send_own(d, a):
        dst = kv_out.at[s, a] if a < 2 else qg_out.at[x, a - 2]
        push(head(a, x + d, zhi), dst, from_x.at[d - 1, a, 0], along_x[d])

    def send_other(d, a):
        push(head(a, x + d, 1 - zhi), oth.at[x, a], from_x.at[d - 1, a, 1], along_x[d])

    def at(zz, r, a, cc=c):
        return kv_out.at[index(zz, x + r, cc), a]

    def forward(src, dst, m, r, a):
        push(src, dst, from_pair.at[m, r, a], to_pair)
        push(src, dst, from_core.at[m, r, a], to_core)

    def own(r, a):
        piece = at(z, r, a)
        arrived(piece, from_x.at[3 - r, a, 0])
        forward(piece, piece, 0, r, a)

    def other(r, a):
        src = (x + r) % 4
        arrived(oth.at[src, a], from_x.at[3 - r, a, 1])
        dst = at(z, r, a) if a < 2 else qg_out.at[4 + src, a - 2]
        push(oth.at[src, a], dst, from_mirror.at[r, a], to_mirror)

    def mirrored(r, a):
        piece = at(mirror, r, a)
        arrived(piece, from_mirror.at[r, a])
        forward(piece, piece, 1, r, a)

    def paired(m, r, a):
        piece = at(3 - pair if m else pair, r, a)
        arrived(piece, from_pair.at[m, r, a])
        push(piece, piece, from_core.at[2 + m, r, a], to_core)

    dots = [move(g_ref, g_all), move(o_ref, o_all)]
    greet(along_x[1:] + [to_mirror, to_pair, to_core])
    for a in (0, 1):
        push(head(a, x, zhi), at(z, 0, a), from_pair.at[0, 0, a], to_pair)
        push(head(a, x, 1 - zhi), at(z, 0, a), from_mirror.at[0, a], to_mirror)
        send_own(1, a)
        send_own(3, a)
    for a in (0, 1):
        send_other(1, a)
        send_other(3, a)
        push(head(a, x, zhi), at(z, 0, a), from_core.at[0, 0, a], to_core)
    stores = [move(head(a, x, zhi), at(z, 0, a)) for a in (0, 1)]
    stores += [move(head(a, x, zhi), qg_out.at[x, a - 2]) for a in (2, 3)]
    for a in (0, 1):
        send_other(2, a)
    for a in (0, 1):
        send_own(2, a)
    for a in (2, 3):
        push(head(a, x, 1 - zhi), qg_out.at[4 + x, a - 2], from_mirror.at[0, a], to_mirror)
    for load in dots:
        load.wait()
    ones = jnp.ones((16, 2 * DH), jnp.bfloat16)
    for h in range(8):
        cols = slice(h * DH, (h + 1) * DH)
        terms = g_all[:, cols].astype(jnp.float32) * o_all[:, cols].astype(jnp.float32)
        high = terms.astype(jnp.bfloat16)
        low = (terms - high.astype(jnp.float32)).astype(jnp.bfloat16)
        sums = dot(ones, jnp.concatenate([high, low], axis=1), NT)
        for t in range(4):
            rd_mine[h // 2, h % 2 * 4 + t : h % 2 * 4 + t + 1, :] = sums[
                0:1, t * 128 : (t + 1) * 128
            ]
    own(3, 0)
    own(1, 0)
    mirrored(0, 0)
    own(3, 1)
    own(1, 1)
    mirrored(0, 1)
    rd_load = move(rd_mine.at[x], rd_out.at[x])
    for d in (1, 2, 3):
        push(rd_mine.at[(x + d) % 4], rd_out.at[x], from_rd.at[d], along_x[d])
    for d in (1, 3, 2):
        for a in (2, 3):
            send_other(d, a)
    for d in (1, 3, 2):
        for a in (2, 3):
            send_own(d, a)
    other(3, 0)
    other(1, 0)
    paired(0, 0, 0)
    paired(0, 0, 1)
    other(3, 1)
    other(1, 1)
    paired(0, 3, 0)
    paired(0, 1, 0)
    mirrored(3, 0)
    other(2, 0)
    mirrored(1, 0)
    other(2, 1)
    paired(1, 0, 0)
    paired(0, 3, 1)
    mirrored(3, 1)
    paired(0, 1, 1)
    own(2, 0)
    mirrored(1, 1)
    own(2, 1)
    mirrored(2, 0)
    paired(1, 0, 1)
    other(3, 2)
    other(1, 2)
    mirrored(2, 1)
    other(3, 3)
    other(1, 3)
    rd_load.wait()
    for d in (1, 2, 3):
        arrived(rd_out.at[(x + 4 - d) % 4], from_rd.at[d])
    near, far = pl.ds(0, 4), pl.ds(4, 4)
    push(rd_out.at[near], rd_out.at[far], from_rd.at[0], to_mirror)
    paired(1, 3, 0)
    paired(1, 1, 0)
    other(2, 2)
    other(2, 3)
    paired(1, 3, 1)
    paired(0, 2, 0)
    paired(1, 1, 1)
    paired(0, 2, 1)
    paired(1, 2, 0)
    paired(1, 2, 1)
    for r in (3, 1, 2):
        for a in (2, 3):
            arrived(qg_out.at[(x + r) % 4, a - 2], from_x.at[3 - r, a, 0])
    for r in range(4):
        for a in (0, 1):
            arrived(qg_out.at[4 + (x + r) % 4, a], from_mirror.at[r, 2 + a])
            for m, zz in enumerate((z, mirror, pair, 3 - pair)):
                arrived(at(zz, r, a, core), from_core.at[m, r, a])
    arrived(rd_out.at[far], from_rd.at[0])
    for copy in stores:
        copy.wait()
    for copy in mover.sent:
        copy.wait_send()


def fetch(k, v, q, g, o):
    anywhere = pl.BlockSpec(memory_space=pl.ANY)
    vmem = pl.BlockSpec(memory_space=pltpu.VMEM)
    dma = pltpu.SemaphoreType.DMA
    return pl.pallas_call(
        fetch_kernel,
        out_shape=(
            jax.ShapeDtypeStruct((32, 2, 512, DH), jnp.bfloat16),
            jax.ShapeDtypeStruct((8, 2, 512, DH), jnp.bfloat16),
            jax.ShapeDtypeStruct((8, 8, 128), jnp.float32),
        ),
        in_specs=[pl.BlockSpec(memory_space=pltpu.MemorySpace.HBM)] * 5,
        out_specs=(anywhere, anywhere, vmem),
        scratch_shapes=[
            pltpu.VMEM((4, 4, 512, DH), jnp.bfloat16),
            pltpu.VMEM((4, 8, 128), jnp.float32),
            pltpu.VMEM((512, 1024), jnp.bfloat16),
            pltpu.VMEM((512, 1024), jnp.bfloat16),
            dma((96,)),
            dma((7,)),
            dma((3, 4, 2)),
            dma((2, 4, 2)),
            dma((4, 4)),
            dma((4, 4, 2)),
            dma((4,)),
        ],
        compiler_params=pltpu.CompilerParams(
            collective_id=0, has_side_effects=True, vmem_limit_bytes=FETCH_VMEM
        ),
    )(*(pltpu.with_memory_space_constraint(a, pltpu.MemorySpace.HBM) for a in (k, v, q, g, o)))


def give_kernel(
    dq_ref, dkv_ref, out_ref,
    part, near, far,
    send, local, from_core, from_pair, from_all,
):
    s = lax.axis_index("seq")
    y = lax.axis_index("head")
    z, x, c = s // 8, s // 2 % 4, s % 2
    zhi = z // 2
    mirror, pair, core = 3 - z, z + 1 - 2 * (z % 2), 1 - c
    to_pair = {"seq": index(pair, x, c), "head": y}
    to_core = {"seq": index(z, x, core), "head": y}
    order = (1, 3, 2, 0)

    def owner(m, r, t):
        return {"seq": index(mirror if m else z, x + r, c), "head": (y + t) % 4}

    peers = [
        owner(m, r, t) for m in (0, 1) for r in range(4) for t in range(4) if (m, r, t) != (0, 0, 0)
    ]
    mover = Mover(send, local)
    push, move = mover.push, mover.move
    classes = (3 - pair, pair, mirror, z)
    units = [(cls, r, a) for cls in range(4) for r in order for a in (0, 1)]
    kept = []

    def spread(m, r, src, kind):
        col = pl.ds(pl.multiple_of(y * 1024 + (x * 2 + zhi) * DH, DH), DH)
        for t in order:
            rows = pl.ds(pl.multiple_of((y + t) % 4 * 128, 128), 128)
            piece, dst = src.at[rows], out_ref.at[kind, :, col]
            if (m, r, t) == (0, 0, 0):
                kept.append(move(piece, dst))
            else:
                push(piece, dst, from_all.at[kind, m, r, t], owner(m, r, t))

    def add(dst, terms):
        @pl.loop(0, 4)
        def _(i):
            rows = pl.ds(pl.multiple_of(i * 128, 128), 128)
            total = terms[0][rows, :].astype(jnp.float32)
            for term in terms[1:]:
                total += term[rows, :].astype(jnp.float32)
            dst[rows, :] = total.astype(jnp.bfloat16)

    loads = {}
    for cls in range(4):
        for r in order:
            at = index(classes[cls], x + r, c)
            loads[cls, r] = move(dkv_ref.at[at], part.at[cls, r])
    greet([to_core, to_pair] + peers)

    def cross(cls, r, a):
        away = index(classes[cls], x + r, core)
        push(dkv_ref.at[away, a], near.at[cls, r, a], from_core.at[cls, r, a], to_core)

    for unit in units[:16]:
        cross(*unit)
    for cls, r, a in units[:16]:
        if a == 0:
            loads[cls, r].wait()
        mover.arrived(near.at[cls, r, a], from_core.at[cls, r, a], to_core)
        mine = part.at[cls, r, a]
        add(mine, (mine, near.at[cls, r, a]))
        push(mine, far.at[cls, r, a], from_pair.at[cls, r, a], to_pair)
        if (cls, r, a) == units[3]:
            for unit in units[16:]:
                cross(*unit)
            for m in (1, 0):
                for rr in order:
                    spread(m, rr, dq_ref.at[m * 4 + (x + rr) % 4], 0)
    for cls, r, a in units[16:]:
        if a == 0:
            loads[cls, r].wait()
        mover.arrived(near.at[cls, r, a], from_core.at[cls, r, a], to_core)
        mover.arrived(far.at[cls - 2, r, a], from_pair.at[cls - 2, r, a], to_pair)
        mine = part.at[cls, r, a]
        add(mine, (mine, near.at[cls, r, a], far.at[cls - 2, r, a]))
        spread(3 - cls, r, mine, 1 + a)
    for m in (0, 1):
        for r in range(4):
            for t in range(4):
                if (m, r, t) == (0, 0, 0):
                    continue
                from_head = (x + 4 - r) % 4 * 2 + (1 - zhi if m else zhi)
                col = pl.multiple_of((y + 4 - t) % 4 * 1024 + from_head * DH, DH)
                for kind in range(3):
                    piece = out_ref.at[kind, :, pl.ds(col, DH)]
                    mover.arrived(piece, from_all.at[kind, m, r, t], to_core)
    for copy in kept:
        copy.wait()
    for copy in mover.sent:
        copy.wait_send()


def give(dq, dkv):
    anywhere = pl.BlockSpec(memory_space=pl.ANY)
    dma = pltpu.SemaphoreType.DMA
    return pl.pallas_call(
        give_kernel,
        out_shape=jax.ShapeDtypeStruct((3, 128, 4096), jnp.bfloat16),
        in_specs=[anywhere] * 2,
        out_specs=anywhere,
        scratch_shapes=[
            pltpu.VMEM((4, 4, 2, 512, DH), jnp.bfloat16),
            pltpu.VMEM((4, 4, 2, 512, DH), jnp.bfloat16),
            pltpu.VMEM((2, 4, 2, 512, DH), jnp.bfloat16),
            dma((144,)),
            dma((19,)),
            dma((4, 4, 2)),
            dma((2, 4, 2)),
            dma((3, 2, 4, 4)),
        ],
        compiler_params=pltpu.CompilerParams(
            collective_id=1, has_side_effects=True, vmem_limit_bytes=GIVE_VMEM
        ),
    )(dq, dkv)


def attend_kernel(
    rand, glob, qg_ref, rd_ref, kv_ref, dq_ref, dkv_ref,
    tab, edge, acc_ref, s0, s1, w0, w1, d0, d1, p0, p1,
):
    s = lax.axis_index("seq")
    z, x, c = s // 8, s // 2 % 4, s % 2
    head = x * 2 + z // 2

    def slot(block):
        return 2 * block - block % 8

    @pl.loop(0, 32)
    def _(i):
        acc_ref[pl.ds(i * 16, 16)] = jnp.zeros((16, BS, DH), jnp.float32)
        shard = jnp.where(i < 16, z, 3 - z) * 8 + i // 4 % 4 * 2 + c
        for u in range(2):
            block = shard * 8 + i % 4 * 2 + u
            at = i * 2 + u
            tab[at * 8] = slot(jnp.maximum(block - 1, 0))
            tab[at * 8 + 1] = slot(block)
            tab[at * 8 + 2] = slot(jnp.minimum(block + 1, 255))
            for j in range(3):
                tab[at * 8 + 3 + j] = slot(rand[j, head, block])
            for j in range(2):
                tab[at * 8 + 6 + j] = slot(glob[j])
            edge[at] = jnp.where(block == 0, 1, jnp.where(block == 255, 2, 0))

    first = lax.broadcasted_iota(jnp.int32, (1, 2 * BS), 1) < BS
    half = z // 2 * 4

    def slots_of(p):
        return [tab[p * 16 + j] for j in range(16)]

    def base_of(p):
        return p // 4 * 16 + p % 4 * 2

    def pair_rows(base):
        a, b = qg_ref[base], qg_ref[base + 1]
        zero = jnp.zeros_like(a)
        return jnp.concatenate(
            [jnp.concatenate([a, zero], axis=1), jnp.concatenate([zero, b], axis=1)], axis=0
        )

    def pair_keys(slots, offset):
        return jnp.concatenate(
            [
                jnp.concatenate([kv_ref[slots[j] + offset], kv_ref[slots[8 + j] + offset]], axis=1)
                for j in range(8)
            ],
            axis=0,
        )

    def score(p, s_ref, w_ref):
        slots, base = slots_of(p), base_of(p)
        s_ref[...] = dot(pair_keys(slots, 0), pair_rows(base), NT)
        w_ref[...] = dot(pair_keys(slots, 8), pair_rows(base + 8), NT)

    def soften(p, s_ref, w_ref, d_ref, p_ref):
        state = jnp.where(first, edge[2 * p], edge[2 * p + 1])
        low = jnp.where(state == 1, -jnp.inf, 0.0)
        high = jnp.where(state == 2, -jnp.inf, 0.0)
        s = s_ref[...] * SCALE_LOG2E
        s = jnp.concatenate(
            [s[:BS] + low, s[BS : 2 * BS], s[2 * BS : 3 * BS] + high, s[3 * BS :]], axis=0
        )
        e = jnp.exp2(s - jnp.max(s, axis=0, keepdims=True))
        weights = e * (1.0 / jnp.sum(e, axis=0, keepdims=True))
        p_ref[...] = weights.astype(jnp.bfloat16)
        rd = rd_ref[p // 4, pl.ds(half + p % 4, 1), :]
        d_ref[...] = (weights * (w_ref[...] - rd)).astype(jnp.bfloat16)

    def spread(p, d_ref, p_ref):
        slots, base = slots_of(p), base_of(p)
        d = d_ref[...]
        dq = dot(d, pair_keys(slots, 0), TN) * SCALE
        dq_ref[2 * p] = dq[:BS, :DH].astype(jnp.bfloat16)
        dq_ref[2 * p + 1] = dq[BS:, DH:].astype(jnp.bfloat16)
        dk = dot(d, pair_rows(base), NN)
        dv = dot(p_ref[...], pair_rows(base + 8), NN)
        for j in range(16):
            side, row = j // 8 * DH, j % 8 * BS
            acc_ref[slots[j]] += dk[row : row + BS, side : side + DH]
            acc_ref[slots[j] + 8] += dv[row : row + BS, side : side + DH]

    score(0, s0, w0)
    soften(0, s0, w0, d0, p0)
    score(1, s1, w1)

    @pl.loop(1, 16)
    def _(t):
        a = 2 * t
        spread(a - 2, d0, p0)
        soften(a - 1, s1, w1, d1, p1)
        score(a, s0, w0)
        spread(a - 1, d1, p1)
        soften(a, s0, w0, d0, p0)
        score(a + 1, s1, w1)

    soften(31, s1, w1, d1, p1)
    spread(30, d0, p0)
    spread(31, d1, p1)

    @pl.loop(0, 32)
    def _(t):
        keys, values = pl.ds(t * 16, 8), pl.ds(t * 16 + 8, 8)
        dkv_ref[keys] = (acc_ref[keys] * SCALE).astype(jnp.bfloat16)
        dkv_ref[values] = acc_ref[values].astype(jnp.bfloat16)


def attend(rand, glob, qg, rd, kv):
    vmem = pl.BlockSpec(memory_space=pltpu.VMEM)
    smem = pl.BlockSpec(memory_space=pltpu.SMEM)
    return pl.pallas_call(
        attend_kernel,
        out_shape=(
            jax.ShapeDtypeStruct((64, BS, DH), jnp.bfloat16),
            jax.ShapeDtypeStruct((512, BS, DH), jnp.bfloat16),
        ),
        in_specs=[smem, smem, vmem, vmem, vmem],
        out_specs=(vmem, vmem),
        scratch_shapes=[
            pltpu.SMEM((512,), jnp.int32),
            pltpu.SMEM((64,), jnp.int32),
            pltpu.VMEM((512, BS, DH), jnp.float32),
        ]
        + [pltpu.VMEM((8 * BS, 2 * BS), jnp.float32)] * 4
        + [pltpu.VMEM((8 * BS, 2 * BS), jnp.bfloat16)] * 4,
        compiler_params=pltpu.CompilerParams(vmem_limit_bytes=ATTEND_VMEM),
    )(rand, glob, qg, rd, kv)


def on_device(
    queries, key_states, value_states, forward_out, grad_out, random_blocks, global_blocks
):
    kv, qg, rd = fetch(key_states, value_states, queries, grad_out, forward_out)
    dq, dkv = attend(
        random_blocks.transpose(2, 1, 0),
        global_blocks,
        qg.reshape(128, BS, DH),
        rd,
        kv.reshape(512, BS, DH),
    )
    outs = give(dq.reshape(8, 512, DH), dkv.reshape(32, 2, 512, DH))
    return outs[0], outs[1], outs[2]


def solution(mesh):
    return jax.shard_map(
        on_device,
        mesh=mesh,
        in_specs=(
            P("seq", "head"),
            P("seq", "head"),
            P("seq", "head"),
            P("seq", "head"),
            P("seq", "head"),
            P(None, "head", None),
            P(),
        ),
        out_specs=(P(("seq", "head"), None), P(("seq", "head"), None), P(("seq", "head"), None)),
        check_vma=False,
    )
```

```python
import jax
import jax.numpy as jnp
from jax import lax
from jax.experimental import pallas as pl
from jax.experimental.pallas import tpu as pltpu
from jax.sharding import PartitionSpec as P

DH = 128
BS = 64
SCALE = DH**-0.5
SCALE_LOG2E = SCALE * 1.4426950408889634
ATTEND_VMEM = 8 * 1024 * 1024
FETCH_VMEM = 10 * 1024 * 1024
GIVE_VMEM = 20 * 1024 * 1024
NT = (((1,), (1,)), ((), ()))
TN = (((0,), (0,)), ((), ()))
NN = (((1,), (0,)), ((), ()))


def dot(a, b, dims):
    return lax.dot_general(a, b, dims, preferred_element_type=jnp.float32)


MESH = pl.DeviceIdType.MESH


def index(z, x, c):
    return z * 8 + x % 4 * 2 + c


class Mover:
    def __init__(self, send, local):
        self.send, self.local = send, local
        self.sent, self.moved = [], []

    def push(self, src, dst, sem, peer):
        copy = pltpu.make_async_remote_copy(
            src_ref=src,
            dst_ref=dst,
            send_sem=self.send.at[len(self.sent)],
            recv_sem=sem,
            device_id=peer,
            device_id_type=MESH,
        )
        copy.start()
        self.sent.append(copy)

    def arrived(self, dst, sem, peer):
        pltpu.make_async_remote_copy(
            src_ref=dst,
            dst_ref=dst,
            send_sem=self.send.at[0],
            recv_sem=sem,
            device_id=peer,
            device_id_type=MESH,
        ).wait_recv()

    def move(self, src, dst):
        copy = pltpu.make_async_copy(src, dst, self.local.at[len(self.moved)])
        copy.start()
        self.moved.append(copy)
        return copy


def welcome(peers):
    barrier = pltpu.get_barrier_semaphore()
    for peer in peers:
        pl.semaphore_signal(barrier, inc=1, device_id=peer, device_id_type=MESH)


def enter(peers):
    pl.semaphore_wait(pltpu.get_barrier_semaphore(), len(peers))


def fetch_kernel(
    k_ref, v_ref, q_ref, g_ref, o_ref,
    kv_out, qg_out, rd_out, zeros,
    oth, rd_mine, g_all, o_all,
    send, local, from_x, from_pair, from_mirror, from_core, from_rd,
):
    s = lax.axis_index("seq")
    z, x, c = s // 8, s // 2 % 4, s % 2
    zhi = z // 2
    mirror, pair, core = 3 - z, z + 1 - 2 * (z % 2), 1 - c
    to_mirror = {"seq": index(mirror, x, c)}
    to_pair = {"seq": index(pair, x, c)}
    to_core = {"seq": index(z, x, core)}
    along_x = [{"seq": index(z, x + d, c)} for d in range(4)]
    mover = Mover(send, local)
    push, move = mover.push, mover.move

    def arrived(dst, sem):
        mover.arrived(dst, sem, to_core)

    ins = (k_ref, v_ref, q_ref, g_ref)

    def head(a, xx, half):
        return ins[a].at[:, pl.ds(pl.multiple_of(xx % 4 * 256 + half * DH, DH), DH)]

    def send_own(d, a):
        dst = kv_out.at[s, a] if a < 2 else qg_out.at[x, a - 2]
        push(head(a, x + d, zhi), dst, from_x.at[d - 1, a, 0], along_x[d])

    def send_other(d, a):
        push(head(a, x + d, 1 - zhi), oth.at[x, a], from_x.at[d - 1, a, 1], along_x[d])

    def at(zz, r, a, cc=c):
        return kv_out.at[index(zz, x + r, cc), a]

    def forward(src, dst, m, r, a):
        push(src, dst, from_pair.at[m, r, a], to_pair)
        push(src, dst, from_core.at[m, r, a], to_core)

    def own(r, a):
        piece = at(z, r, a)
        arrived(piece, from_x.at[3 - r, a, 0])
        forward(piece, piece, 0, r, a)

    def other(r, a):
        src = (x + r) % 4
        arrived(oth.at[src, a], from_x.at[3 - r, a, 1])
        dst = at(z, r, a) if a < 2 else qg_out.at[4 + src, a - 2]
        push(oth.at[src, a], dst, from_mirror.at[r, a], to_mirror)

    def mirrored(r, a):
        piece = at(mirror, r, a)
        arrived(piece, from_mirror.at[r, a])
        forward(piece, piece, 1, r, a)

    def paired(m, r, a):
        piece = at(3 - pair if m else pair, r, a)
        arrived(piece, from_pair.at[m, r, a])
        push(piece, piece, from_core.at[2 + m, r, a], to_core)

    dots = [move(g_ref, g_all), move(o_ref, o_all)]
    welcome(along_x[1:] + [to_mirror, to_pair, to_core])
    enter(along_x[1:] + [to_mirror, to_pair, to_core])
    for a in (0, 1):
        push(head(a, x, zhi), at(z, 0, a), from_pair.at[0, 0, a], to_pair)
        push(head(a, x, 1 - zhi), at(z, 0, a), from_mirror.at[0, a], to_mirror)
        send_own(1, a)
        send_own(3, a)
    for a in (0, 1):
        send_other(1, a)
        send_other(3, a)
        push(head(a, x, zhi), at(z, 0, a), from_core.at[0, 0, a], to_core)
    stores = [move(head(a, x, zhi), at(z, 0, a)) for a in (0, 1)]
    stores += [move(head(a, x, zhi), qg_out.at[x, a - 2]) for a in (2, 3)]
    for a in (0, 1):
        send_other(2, a)
    for a in (0, 1):
        send_own(2, a)
    for a in (2, 3):
        push(head(a, x, 1 - zhi), qg_out.at[4 + x, a - 2], from_mirror.at[0, a], to_mirror)
    for load in dots:
        load.wait()
    ones = jnp.ones((16, 2 * DH), jnp.bfloat16)
    for h in range(8):
        cols = slice(h * DH, (h + 1) * DH)
        terms = g_all[:, cols].astype(jnp.float32) * o_all[:, cols].astype(jnp.float32)
        high = terms.astype(jnp.bfloat16)
        low = (terms - high.astype(jnp.float32)).astype(jnp.bfloat16)
        sums = dot(ones, jnp.concatenate([high, low], axis=1), NT)
        for t in range(4):
            rd_mine[h // 2, h % 2 * 4 + t : h % 2 * 4 + t + 1, :] = sums[
                0:1, t * 128 : (t + 1) * 128
            ]
    own(3, 0)
    own(1, 0)
    mirrored(0, 0)
    own(3, 1)
    own(1, 1)
    mirrored(0, 1)
    rd_load = move(rd_mine.at[x], rd_out.at[x])
    for d in (1, 2, 3):
        push(rd_mine.at[(x + d) % 4], rd_out.at[x], from_rd.at[d], along_x[d])
    for d in (1, 3, 2):
        for a in (2, 3):
            send_other(d, a)
    for d in (1, 3, 2):
        for a in (2, 3):
            send_own(d, a)
    other(3, 0)
    other(1, 0)
    paired(0, 0, 0)
    paired(0, 0, 1)
    other(3, 1)
    other(1, 1)
    paired(0, 3, 0)
    paired(0, 1, 0)
    mirrored(3, 0)
    other(2, 0)
    mirrored(1, 0)
    other(2, 1)
    paired(1, 0, 0)
    paired(0, 3, 1)
    mirrored(3, 1)
    paired(0, 1, 1)
    own(2, 0)
    mirrored(1, 1)
    own(2, 1)
    mirrored(2, 0)
    paired(1, 0, 1)
    other(3, 2)
    other(1, 2)
    mirrored(2, 1)
    other(3, 3)
    other(1, 3)
    rd_load.wait()
    for d in (1, 2, 3):
        arrived(rd_out.at[(x + 4 - d) % 4], from_rd.at[d])
    near, far = pl.ds(0, 4), pl.ds(4, 4)
    push(rd_out.at[near], rd_out.at[far], from_rd.at[0], to_mirror)
    paired(1, 3, 0)
    paired(1, 1, 0)
    other(2, 2)
    other(2, 3)

    @pl.loop(0, 32)
    def _(i):
        zeros[pl.ds(i * 16, 16)] = jnp.zeros((16, BS, DH), jnp.float32)

    paired(1, 3, 1)
    paired(0, 2, 0)
    paired(1, 1, 1)
    paired(0, 2, 1)
    paired(1, 2, 0)
    paired(1, 2, 1)
    for r in (3, 1, 2):
        for a in (2, 3):
            arrived(qg_out.at[(x + r) % 4, a - 2], from_x.at[3 - r, a, 0])
    for r in range(4):
        for a in (0, 1):
            arrived(qg_out.at[4 + (x + r) % 4, a], from_mirror.at[r, 2 + a])
            for m, zz in enumerate((z, mirror, pair, 3 - pair)):
                arrived(at(zz, r, a, core), from_core.at[m, r, a])
    arrived(rd_out.at[far], from_rd.at[0])
    for copy in stores:
        copy.wait()
    for copy in mover.sent:
        copy.wait_send()


def fetch(k, v, q, g, o):
    anywhere = pl.BlockSpec(memory_space=pl.ANY)
    vmem = pl.BlockSpec(memory_space=pltpu.VMEM)
    dma = pltpu.SemaphoreType.DMA
    return pl.pallas_call(
        fetch_kernel,
        out_shape=(
            jax.ShapeDtypeStruct((32, 2, 512, DH), jnp.bfloat16),
            jax.ShapeDtypeStruct((8, 2, 512, DH), jnp.bfloat16),
            jax.ShapeDtypeStruct((8, 8, 128), jnp.float32),
            jax.ShapeDtypeStruct((512, BS, DH), jnp.float32),
        ),
        in_specs=[pl.BlockSpec(memory_space=pltpu.MemorySpace.HBM)] * 5,
        out_specs=(anywhere, anywhere, vmem, vmem),
        scratch_shapes=[
            pltpu.VMEM((4, 4, 512, DH), jnp.bfloat16),
            pltpu.VMEM((4, 8, 128), jnp.float32),
            pltpu.VMEM((512, 1024), jnp.bfloat16),
            pltpu.VMEM((512, 1024), jnp.bfloat16),
            dma((96,)),
            dma((7,)),
            dma((3, 4, 2)),
            dma((2, 4, 2)),
            dma((4, 4)),
            dma((4, 4, 2)),
            dma((4,)),
        ],
        compiler_params=pltpu.CompilerParams(
            collective_id=0, has_side_effects=True, vmem_limit_bytes=FETCH_VMEM
        ),
    )(*(pltpu.with_memory_space_constraint(a, pltpu.MemorySpace.HBM) for a in (k, v, q, g, o)))


def give_kernel(
    dq_ref, acc_ref, out_ref,
    part, away, near, far,
    send, local, from_core, from_pair, from_all,
):
    s = lax.axis_index("seq")
    y = lax.axis_index("head")
    z, x, c = s // 8, s // 2 % 4, s % 2
    zhi = z // 2
    mirror, pair, core = 3 - z, z + 1 - 2 * (z % 2), 1 - c
    to_pair = {"seq": index(pair, x, c), "head": y}
    to_core = {"seq": index(z, x, core), "head": y}
    order = (2, 1, 3, 0)

    def owner(m, r, t):
        return {"seq": index(mirror if m else z, x + r, c), "head": (y + t) % 4}

    peers = [
        owner(m, r, t) for m in (0, 1) for r in range(4) for t in range(4) if (m, r, t) != (0, 0, 0)
    ]
    mover = Mover(send, local)
    push, move = mover.push, mover.move
    classes = (3 - pair, pair, mirror, z)
    units = [(cls, r, a) for cls in range(4) for r in order for a in (0, 1)]
    kept = []

    def spread(m, r, src, kind):
        col = pl.ds(pl.multiple_of(y * 1024 + (x * 2 + zhi) * DH, DH), DH)
        for t in order:
            rows = pl.ds(pl.multiple_of((y + t) % 4 * 128, 128), 128)
            piece, dst = src.at[rows], out_ref.at[kind, :, col]
            if (m, r, t) == (0, 0, 0):
                kept.append(move(piece, dst))
            else:
                push(piece, dst, from_all.at[kind, m, r, t], owner(m, r, t))

    def add(dst, slot, a, terms):
        @pl.loop(0, 4)
        def _(i):
            rows = pl.ds(pl.multiple_of(i * 128, 128), 128)
            total = acc_ref[slot, a, rows, :]
            if a == 0:
                total *= SCALE
            for term in terms:
                total += term[rows, :].astype(jnp.float32)
            dst[rows, :] = total.astype(jnp.bfloat16)

    def leave(cls, r, a):
        add(away.at[cls, r, a], index(classes[cls], x + r, core), a, ())

    def cross(cls, r, a):
        sem = from_core.at[cls, r, a]
        push(away.at[cls, r, a], near.at[cls, r, a], sem, to_core)

    welcome([to_core, to_pair] + peers)
    for unit in units[:16]:
        leave(*unit)
    enter([to_core, to_pair] + peers)
    for unit in units[:16]:
        cross(*unit)
    for cls, r, a in units[:16]:
        mover.arrived(near.at[cls, r, a], from_core.at[cls, r, a], to_core)
        mine = part.at[cls, r, a]
        add(mine, index(classes[cls], x + r, c), a, (near.at[cls, r, a],))
        push(mine, far.at[cls, r, a], from_pair.at[cls, r, a], to_pair)
        if (cls, r, a) == units[3]:
            for m in (1, 0):
                for rr in order:
                    spread(m, rr, dq_ref.at[m * 4 + (x + rr) % 4], 0)
            for unit in units[16:]:
                leave(*unit)
                cross(*unit)
    for cls, r, a in units[16:]:
        mover.arrived(near.at[cls, r, a], from_core.at[cls, r, a], to_core)
        mover.arrived(far.at[cls - 2, r, a], from_pair.at[cls - 2, r, a], to_pair)
        mine = part.at[cls, r, a]
        terms = (near.at[cls, r, a], far.at[cls - 2, r, a])
        add(mine, index(classes[cls], x + r, c), a, terms)
        spread(3 - cls, r, mine, 1 + a)
    for m in (0, 1):
        for r in range(4):
            for t in range(4):
                if (m, r, t) == (0, 0, 0):
                    continue
                from_head = (x + 4 - r) % 4 * 2 + (1 - zhi if m else zhi)
                col = pl.multiple_of((y + 4 - t) % 4 * 1024 + from_head * DH, DH)
                for kind in range(3):
                    piece = out_ref.at[kind, :, pl.ds(col, DH)]
                    mover.arrived(piece, from_all.at[kind, m, r, t], to_core)
    for copy in kept:
        copy.wait()
    for copy in mover.sent:
        copy.wait_send()


def give(dq, acc):
    anywhere = pl.BlockSpec(memory_space=pl.ANY)
    dma = pltpu.SemaphoreType.DMA
    return pl.pallas_call(
        give_kernel,
        out_shape=jax.ShapeDtypeStruct((3, 128, 4096), jnp.bfloat16),
        in_specs=[anywhere, pl.BlockSpec(memory_space=pltpu.VMEM)],
        out_specs=anywhere,
        scratch_shapes=[
            pltpu.VMEM((4, 4, 2, 512, DH), jnp.bfloat16),
            pltpu.VMEM((4, 4, 2, 512, DH), jnp.bfloat16),
            pltpu.VMEM((4, 4, 2, 512, DH), jnp.bfloat16),
            pltpu.VMEM((2, 4, 2, 512, DH), jnp.bfloat16),
            dma((144,)),
            dma((3,)),
            dma((4, 4, 2)),
            dma((2, 4, 2)),
            dma((3, 2, 4, 4)),
        ],
        compiler_params=pltpu.CompilerParams(
            collective_id=1, has_side_effects=True, vmem_limit_bytes=GIVE_VMEM
        ),
    )(dq, acc)


def attend_kernel(
    rand, glob, qg_ref, rd_ref, kv_ref, zeros_ref, dq_ref, acc_ref,
    s0, s1, w0, w1, d0, d1, p0, p1,
):
    s = lax.axis_index("seq")
    z, x, c = s // 8, s // 2 % 4, s % 2
    head = x * 2 + z // 2
    first = lax.broadcasted_iota(jnp.int32, (1, 2 * BS), 1) < BS
    half = z // 2 * 4

    def block_of(p):
        shard = jnp.where(p < 16, z, 3 - z) * 8 + p // 4 % 4 * 2 + c
        return shard * 8 + p % 4 * 2

    def slots_of(p):
        slots = []
        for block in (block_of(p), block_of(p) + 1):
            named = [jnp.maximum(block - 1, 0), block, jnp.minimum(block + 1, 255)]
            named += [rand[j, head, block] for j in range(3)] + [glob[0], glob[1]]
            slots += [2 * b - b % 8 for b in named]
        return slots

    def base_of(p):
        return p // 4 * 16 + p % 4 * 2

    def pair_rows(base):
        a, b = qg_ref[base], qg_ref[base + 1]
        zero = jnp.zeros_like(a)
        return jnp.concatenate(
            [jnp.concatenate([a, zero], axis=1), jnp.concatenate([zero, b], axis=1)], axis=0
        )

    def pair_keys(slots, offset):
        return jnp.concatenate(
            [
                jnp.concatenate([kv_ref[slots[j] + offset], kv_ref[slots[8 + j] + offset]], axis=1)
                for j in range(8)
            ],
            axis=0,
        )

    def score(p, s_ref, w_ref):
        slots, base = slots_of(p), base_of(p)
        s_ref[...] = dot(pair_keys(slots, 0), pair_rows(base), NT)
        w_ref[...] = dot(pair_keys(slots, 8), pair_rows(base + 8), NT)

    def soften(p, s_ref, w_ref, d_ref, p_ref):
        low = jnp.where(first & (block_of(p) == 0), -jnp.inf, 0.0)
        high = jnp.where(~first & (block_of(p) == 254), -jnp.inf, 0.0)
        s = s_ref[...] * SCALE_LOG2E
        s = jnp.concatenate(
            [s[:BS] + low, s[BS : 2 * BS], s[2 * BS : 3 * BS] + high, s[3 * BS :]], axis=0
        )
        e = jnp.exp2(s - jnp.max(s, axis=0, keepdims=True))
        weights = e * (1.0 / jnp.sum(e, axis=0, keepdims=True))
        p_ref[...] = weights.astype(jnp.bfloat16)
        rd = rd_ref[p // 4, pl.ds(half + p % 4, 1), :]
        d_ref[...] = (weights * (w_ref[...] - rd)).astype(jnp.bfloat16)

    def spread(p, d_ref, p_ref):
        slots, base = slots_of(p), base_of(p)
        d = d_ref[...]
        dq = dot(d, pair_keys(slots, 0), TN) * SCALE
        dq_ref[2 * p] = dq[:BS, :DH].astype(jnp.bfloat16)
        dq_ref[2 * p + 1] = dq[BS:, DH:].astype(jnp.bfloat16)
        dk = dot(d, pair_rows(base), NN)
        dv = dot(p_ref[...], pair_rows(base + 8), NN)
        for j in range(16):
            side, row = j // 8 * DH, j % 8 * BS
            acc_ref[slots[j]] += dk[row : row + BS, side : side + DH]
            acc_ref[slots[j] + 8] += dv[row : row + BS, side : side + DH]

    score(0, s0, w0)
    soften(0, s0, w0, d0, p0)
    score(1, s1, w1)

    @pl.loop(1, 16)
    def _(t):
        a = 2 * t
        spread(a - 2, d0, p0)
        soften(a - 1, s1, w1, d1, p1)
        score(a, s0, w0)
        spread(a - 1, d1, p1)
        soften(a, s0, w0, d0, p0)
        score(a + 1, s1, w1)

    soften(31, s1, w1, d1, p1)
    spread(30, d0, p0)
    spread(31, d1, p1)


def attend(rand, glob, qg, rd, kv, zeros):
    vmem = pl.BlockSpec(memory_space=pltpu.VMEM)
    smem = pl.BlockSpec(memory_space=pltpu.SMEM)
    return pl.pallas_call(
        attend_kernel,
        out_shape=(
            jax.ShapeDtypeStruct((64, BS, DH), jnp.bfloat16),
            jax.ShapeDtypeStruct((512, BS, DH), jnp.float32),
        ),
        in_specs=[smem, smem, vmem, vmem, vmem, vmem],
        out_specs=(vmem, vmem),
        input_output_aliases={5: 1},
        scratch_shapes=[pltpu.VMEM((8 * BS, 2 * BS), jnp.float32)] * 4
        + [pltpu.VMEM((8 * BS, 2 * BS), jnp.bfloat16)] * 4,
        compiler_params=pltpu.CompilerParams(vmem_limit_bytes=ATTEND_VMEM),
    )(
        *(pltpu.with_memory_space_constraint(a, pltpu.MemorySpace.HBM) for a in (rand, glob)),
        qg,
        rd,
        kv,
        zeros,
    )


def on_device(
    queries, key_states, value_states, forward_out, grad_out, random_blocks, global_blocks
):
    kv, qg, rd, zeros = fetch(key_states, value_states, queries, grad_out, forward_out)
    dq, acc = attend(
        random_blocks.transpose(2, 1, 0),
        global_blocks,
        qg.reshape(128, BS, DH),
        rd,
        kv.reshape(512, BS, DH),
        zeros,
    )
    outs = give(dq.reshape(8, 512, DH), acc.reshape(32, 2, 512, DH))
    return outs[0], outs[1], outs[2]


def solution(mesh):
    return jax.shard_map(
        on_device,
        mesh=mesh,
        in_specs=(
            P("seq", "head"),
            P("seq", "head"),
            P("seq", "head"),
            P("seq", "head"),
            P("seq", "head"),
            P(None, "head", None),
            P(),
        ),
        out_specs=(P(("seq", "head"), None), P(("seq", "head"), None), P(("seq", "head"), None)),
        check_vma=False,
    )
```

```python
import jax
import jax.numpy as jnp
from jax import lax
from jax.experimental import pallas as pl
from jax.experimental.pallas import tpu as pltpu
from jax.sharding import PartitionSpec as P

DH = 128
BS = 64
SCALE = DH**-0.5
SCALE_LOG2E = SCALE * 1.4426950408889634
ATTEND_VMEM = 8 * 1024 * 1024
FETCH_VMEM = 10 * 1024 * 1024
GIVE_VMEM = 20 * 1024 * 1024
NT = (((1,), (1,)), ((), ()))
TN = (((0,), (0,)), ((), ()))
NN = (((1,), (0,)), ((), ()))


def dot(a, b, dims):
    return lax.dot_general(a, b, dims, preferred_element_type=jnp.float32)


MESH = pl.DeviceIdType.MESH


def index(z, x, c):
    return z * 8 + x % 4 * 2 + c


class Mover:
    def __init__(self, send, local):
        self.send, self.local = send, local
        self.sent, self.moved = [], []

    def push(self, src, dst, sem, peer):
        copy = pltpu.make_async_remote_copy(
            src_ref=src,
            dst_ref=dst,
            send_sem=self.send.at[len(self.sent)],
            recv_sem=sem,
            device_id=peer,
            device_id_type=MESH,
        )
        copy.start()
        self.sent.append(copy)

    def arrived(self, dst, sem, peer):
        pltpu.make_async_remote_copy(
            src_ref=dst,
            dst_ref=dst,
            send_sem=self.send.at[0],
            recv_sem=sem,
            device_id=peer,
            device_id_type=MESH,
        ).wait_recv()

    def move(self, src, dst):
        copy = pltpu.make_async_copy(src, dst, self.local.at[len(self.moved)])
        copy.start()
        self.moved.append(copy)
        return copy


def welcome(peers):
    barrier = pltpu.get_barrier_semaphore()
    for peer in peers:
        pl.semaphore_signal(barrier, inc=1, device_id=peer, device_id_type=MESH)


def enter(peers):
    pl.semaphore_wait(pltpu.get_barrier_semaphore(), len(peers))


def fetch_kernel(
    k_ref, v_ref, q_ref, g_ref, o_ref,
    kv_out, qg_out, rd_out, zeros,
    oth, rd_mine, g_all, o_all,
    send, local, from_x, from_pair, from_mirror, from_core, from_rd,
):
    s = lax.axis_index("seq")
    z, x, c = s // 8, s // 2 % 4, s % 2
    zhi = z // 2
    mirror, pair, core = 3 - z, z + 1 - 2 * (z % 2), 1 - c
    to_mirror = {"seq": index(mirror, x, c)}
    to_pair = {"seq": index(pair, x, c)}
    to_core = {"seq": index(z, x, core)}
    along_x = [{"seq": index(z, x + d, c)} for d in range(4)]
    mover = Mover(send, local)
    push, move = mover.push, mover.move

    def arrived(dst, sem):
        mover.arrived(dst, sem, to_core)

    ins = (k_ref, v_ref, q_ref, g_ref)

    def head(a, xx, half):
        return ins[a].at[:, pl.ds(pl.multiple_of(xx % 4 * 256 + half * DH, DH), DH)]

    def send_own(d, a):
        dst = kv_out.at[s, a] if a < 2 else qg_out.at[x, a - 2]
        push(head(a, x + d, zhi), dst, from_x.at[d - 1, a, 0], along_x[d])

    def send_other(d, a):
        push(head(a, x + d, 1 - zhi), oth.at[x, a], from_x.at[d - 1, a, 1], along_x[d])

    def at(zz, r, a, cc=c):
        return kv_out.at[index(zz, x + r, cc), a]

    def forward(src, dst, m, r, a):
        push(src, dst, from_pair.at[m, r, a], to_pair)
        push(src, dst, from_core.at[m, r, a], to_core)

    def own(r, a):
        piece = at(z, r, a)
        arrived(piece, from_x.at[3 - r, a, 0])
        forward(piece, piece, 0, r, a)

    def other(r, a):
        src = (x + r) % 4
        arrived(oth.at[src, a], from_x.at[3 - r, a, 1])
        dst = at(z, r, a) if a < 2 else qg_out.at[4 + src, a - 2]
        push(oth.at[src, a], dst, from_mirror.at[r, a], to_mirror)

    def mirrored(r, a):
        piece = at(mirror, r, a)
        arrived(piece, from_mirror.at[r, a])
        forward(piece, piece, 1, r, a)

    def paired(m, r, a):
        piece = at(3 - pair if m else pair, r, a)
        arrived(piece, from_pair.at[m, r, a])
        push(piece, piece, from_core.at[2 + m, r, a], to_core)

    dots = [move(g_ref, g_all), move(o_ref, o_all)]
    welcome(along_x[1:] + [to_mirror, to_pair, to_core])
    enter(along_x[1:] + [to_mirror, to_pair, to_core])
    for a in (0, 1):
        push(head(a, x, zhi), at(z, 0, a), from_pair.at[0, 0, a], to_pair)
        push(head(a, x, 1 - zhi), at(z, 0, a), from_mirror.at[0, a], to_mirror)
        send_own(1, a)
        send_own(3, a)
    for a in (0, 1):
        send_other(1, a)
        send_other(3, a)
        push(head(a, x, zhi), at(z, 0, a), from_core.at[0, 0, a], to_core)
    stores = [move(head(a, x, zhi), at(z, 0, a)) for a in (0, 1)]
    stores += [move(head(a, x, zhi), qg_out.at[x, a - 2]) for a in (2, 3)]
    for a in (0, 1):
        send_other(2, a)
    for a in (0, 1):
        send_own(2, a)
    for a in (2, 3):
        push(head(a, x, 1 - zhi), qg_out.at[4 + x, a - 2], from_mirror.at[0, a], to_mirror)
    for load in dots:
        load.wait()
    ones = jnp.ones((16, 2 * DH), jnp.bfloat16)
    for h in range(8):
        cols = slice(h * DH, (h + 1) * DH)
        terms = g_all[:, cols].astype(jnp.float32) * o_all[:, cols].astype(jnp.float32)
        high = terms.astype(jnp.bfloat16)
        low = (terms - high.astype(jnp.float32)).astype(jnp.bfloat16)
        sums = dot(ones, jnp.concatenate([high, low], axis=1), NT)
        for t in range(4):
            rd_mine[h // 2, h % 2 * 4 + t : h % 2 * 4 + t + 1, :] = sums[
                0:1, t * 128 : (t + 1) * 128
            ]
    own(3, 0)
    own(1, 0)
    mirrored(0, 0)
    own(3, 1)
    own(1, 1)
    mirrored(0, 1)
    rd_load = move(rd_mine.at[x], rd_out.at[x])
    for d in (1, 2, 3):
        push(rd_mine.at[(x + d) % 4], rd_out.at[x], from_rd.at[d], along_x[d])
    for d in (1, 3, 2):
        for a in (2, 3):
            send_other(d, a)
    for d in (1, 3, 2):
        for a in (2, 3):
            send_own(d, a)
    other(3, 0)
    other(1, 0)
    paired(0, 0, 0)
    paired(0, 0, 1)
    other(3, 1)
    other(1, 1)
    paired(0, 3, 0)
    paired(0, 1, 0)
    mirrored(3, 0)
    other(2, 0)
    mirrored(1, 0)
    other(2, 1)
    paired(1, 0, 0)
    paired(0, 3, 1)
    mirrored(3, 1)
    paired(0, 1, 1)
    own(2, 0)
    mirrored(1, 1)
    own(2, 1)
    mirrored(2, 0)
    paired(1, 0, 1)
    other(3, 2)
    other(1, 2)
    mirrored(2, 1)
    other(3, 3)
    other(1, 3)
    rd_load.wait()
    for d in (1, 2, 3):
        arrived(rd_out.at[(x + 4 - d) % 4], from_rd.at[d])
    near, far = pl.ds(0, 4), pl.ds(4, 4)
    push(rd_out.at[near], rd_out.at[far], from_rd.at[0], to_mirror)
    paired(1, 3, 0)
    paired(1, 1, 0)
    other(2, 2)
    other(2, 3)

    @pl.loop(0, 32)
    def _(i):
        zeros[pl.ds(i * 16, 16)] = jnp.zeros((16, BS, DH), jnp.float32)

    paired(1, 3, 1)
    paired(0, 2, 0)
    paired(1, 1, 1)
    paired(0, 2, 1)
    paired(1, 2, 0)
    paired(1, 2, 1)
    for r in (3, 1, 2):
        for a in (2, 3):
            arrived(qg_out.at[(x + r) % 4, a - 2], from_x.at[3 - r, a, 0])
    for r in range(4):
        for a in (0, 1):
            arrived(qg_out.at[4 + (x + r) % 4, a], from_mirror.at[r, 2 + a])
            for m, zz in enumerate((z, mirror, pair, 3 - pair)):
                arrived(at(zz, r, a, core), from_core.at[m, r, a])
    arrived(rd_out.at[far], from_rd.at[0])
    for copy in stores:
        copy.wait()
    for copy in mover.sent:
        copy.wait_send()


def fetch(k, v, q, g, o):
    anywhere = pl.BlockSpec(memory_space=pl.ANY)
    vmem = pl.BlockSpec(memory_space=pltpu.VMEM)
    dma = pltpu.SemaphoreType.DMA
    return pl.pallas_call(
        fetch_kernel,
        out_shape=(
            jax.ShapeDtypeStruct((32, 2, 512, DH), jnp.bfloat16),
            jax.ShapeDtypeStruct((8, 2, 512, DH), jnp.bfloat16),
            jax.ShapeDtypeStruct((8, 8, 128), jnp.float32),
            jax.ShapeDtypeStruct((512, BS, DH), jnp.float32),
        ),
        in_specs=[pl.BlockSpec(memory_space=pltpu.MemorySpace.HBM)] * 5,
        out_specs=(anywhere, anywhere, vmem, vmem),
        scratch_shapes=[
            pltpu.VMEM((4, 4, 512, DH), jnp.bfloat16),
            pltpu.VMEM((4, 8, 128), jnp.float32),
            pltpu.VMEM((512, 1024), jnp.bfloat16),
            pltpu.VMEM((512, 1024), jnp.bfloat16),
            dma((96,)),
            dma((7,)),
            dma((3, 4, 2)),
            dma((2, 4, 2)),
            dma((4, 4)),
            dma((4, 4, 2)),
            dma((4,)),
        ],
        compiler_params=pltpu.CompilerParams(
            collective_id=0, has_side_effects=True, vmem_limit_bytes=FETCH_VMEM
        ),
    )(*(pltpu.with_memory_space_constraint(a, pltpu.MemorySpace.HBM) for a in (k, v, q, g, o)))


def give_kernel(
    dq_ref, acc_ref, out_ref,
    part, away, near, far,
    send, local, from_core, from_pair, from_last, from_all,
):
    s = lax.axis_index("seq")
    y = lax.axis_index("head")
    z, x, c = s // 8, s // 2 % 4, s % 2
    zhi = z // 2
    mirror, pair, core = 3 - z, z + 1 - 2 * (z % 2), 1 - c
    to_pair = {"seq": index(pair, x, c), "head": y}
    to_core = {"seq": index(z, x, core), "head": y}
    order = (2, 1, 3, 0)

    def owner(m, r, t):
        return {"seq": index(mirror if m else z, x + r, c), "head": (y + t) % 4}

    peers = [
        owner(m, r, t) for m in (0, 1) for r in range(4) for t in range(4) if (m, r, t) != (0, 0, 0)
    ]
    mover = Mover(send, local)
    push, move = mover.push, mover.move
    classes = (3 - pair, pair, mirror, z)
    units = [(cls, r, a) for cls in range(4) for r in order for a in (0, 1)]
    kept = []

    def quarter(t):
        return pl.ds(pl.multiple_of((y + t) % 4 * 128, 128), 128)

    def hand(m, r, t, src, kind):
        col = pl.ds(pl.multiple_of(y * 1024 + (x * 2 + zhi) * DH, DH), DH)
        piece, dst = src.at[quarter(t)], out_ref.at[kind, :, col]
        if (m, r, t) == (0, 0, 0):
            kept.append(move(piece, dst))
        else:
            push(piece, dst, from_all.at[kind, m, r, t], owner(m, r, t))

    def spread(m, r, src, kind):
        for t in order:
            hand(m, r, t, src, kind)

    def add_rows(dst, slot, a, rows, terms):
        total = acc_ref[slot, a, rows, :]
        if a == 0:
            total *= SCALE
        for term in terms:
            total += term[rows, :].astype(jnp.float32)
        dst[rows, :] = total.astype(jnp.bfloat16)

    def add(dst, slot, a, terms):
        @pl.loop(0, 4)
        def _(i):
            rows = pl.ds(pl.multiple_of(i * 128, 128), 128)
            add_rows(dst, slot, a, rows, terms)

    def leave(cls, r, a):
        add(away.at[cls, r, a], index(classes[cls], x + r, core), a, ())

    def cross(cls, r, a):
        sem = from_core.at[cls, r, a]
        push(away.at[cls, r, a], near.at[cls, r, a], sem, to_core)

    welcome([to_core, to_pair] + peers)
    for unit in units[:16]:
        leave(*unit)
    enter([to_core, to_pair] + peers)
    for unit in units[:16]:
        cross(*unit)
    for cls, r, a in units[:14]:
        mover.arrived(near.at[cls, r, a], from_core.at[cls, r, a], to_core)
        mine = part.at[cls, r, a]
        add(mine, index(classes[cls], x + r, c), a, (near.at[cls, r, a],))
        push(mine, far.at[cls, r, a], from_pair.at[cls, r, a], to_pair)
        if (cls, r, a) == units[3]:
            for m in (1, 0):
                for rr in order:
                    spread(m, rr, dq_ref.at[m * 4 + (x + rr) % 4], 0)
            for unit in units[16:]:
                leave(*unit)
                cross(*unit)
    for a in (0, 1):
        mover.arrived(near.at[1, 0, a], from_core.at[1, 0, a], to_core)
    for t in order:
        for a in (0, 1):
            mine, rows = part.at[1, 0, a], quarter(t)
            add_rows(mine, index(pair, x, c), a, rows, (near.at[1, 0, a],))
            push(mine.at[rows], far.at[1, 0, a, rows], from_last.at[a, t], to_pair)
    for cls, r, a in units[16:30]:
        mover.arrived(near.at[cls, r, a], from_core.at[cls, r, a], to_core)
        mover.arrived(far.at[cls - 2, r, a], from_pair.at[cls - 2, r, a], to_pair)
        mine = part.at[cls, r, a]
        terms = (near.at[cls, r, a], far.at[cls - 2, r, a])
        add(mine, index(classes[cls], x + r, c), a, terms)
        spread(3 - cls, r, mine, 1 + a)
    for a in (0, 1):
        mover.arrived(near.at[3, 0, a], from_core.at[3, 0, a], to_core)
    for t in order:
        for a in (0, 1):
            mine, rows = part.at[3, 0, a], quarter(t)
            mover.arrived(far.at[1, 0, a, rows], from_last.at[a, t], to_pair)
            add_rows(mine, index(z, x, c), a, rows, (near.at[3, 0, a], far.at[1, 0, a]))
            hand(0, 0, t, mine, 1 + a)
    for m in (0, 1):
        for r in range(4):
            for t in range(4):
                if (m, r, t) == (0, 0, 0):
                    continue
                from_head = (x + 4 - r) % 4 * 2 + (1 - zhi if m else zhi)
                col = pl.multiple_of((y + 4 - t) % 4 * 1024 + from_head * DH, DH)
                for kind in range(3):
                    piece = out_ref.at[kind, :, pl.ds(col, DH)]
                    mover.arrived(piece, from_all.at[kind, m, r, t], to_core)
    for copy in kept:
        copy.wait()
    for copy in mover.sent:
        copy.wait_send()


def give(dq, acc):
    anywhere = pl.BlockSpec(memory_space=pl.ANY)
    dma = pltpu.SemaphoreType.DMA
    return pl.pallas_call(
        give_kernel,
        out_shape=jax.ShapeDtypeStruct((3, 128, 4096), jnp.bfloat16),
        in_specs=[anywhere, pl.BlockSpec(memory_space=pltpu.VMEM)],
        out_specs=anywhere,
        scratch_shapes=[
            pltpu.VMEM((4, 4, 2, 512, DH), jnp.bfloat16),
            pltpu.VMEM((4, 4, 2, 512, DH), jnp.bfloat16),
            pltpu.VMEM((4, 4, 2, 512, DH), jnp.bfloat16),
            pltpu.VMEM((2, 4, 2, 512, DH), jnp.bfloat16),
            dma((148,)),
            dma((3,)),
            dma((4, 4, 2)),
            dma((2, 4, 2)),
            dma((2, 4)),
            dma((3, 2, 4, 4)),
        ],
        compiler_params=pltpu.CompilerParams(
            collective_id=1, has_side_effects=True, vmem_limit_bytes=GIVE_VMEM
        ),
    )(dq, acc)


def attend_kernel(
    rand, glob, qg_ref, rd_ref, kv_ref, zeros_ref, dq_ref, acc_ref,
    s0, s1, w0, w1, d0, d1, p0, p1,
):
    s = lax.axis_index("seq")
    z, x, c = s // 8, s // 2 % 4, s % 2
    head = x * 2 + z // 2
    first = lax.broadcasted_iota(jnp.int32, (1, 2 * BS), 1) < BS
    half = z // 2 * 4

    def block_of(p):
        shard = jnp.where(p < 16, z, 3 - z) * 8 + p // 4 % 4 * 2 + c
        return shard * 8 + p % 4 * 2

    def slots_of(p):
        slots = []
        for block in (block_of(p), block_of(p) + 1):
            named = [jnp.maximum(block - 1, 0), block, jnp.minimum(block + 1, 255)]
            named += [rand[j, head, block] for j in range(3)] + [glob[0], glob[1]]
            slots += [2 * b - b % 8 for b in named]
        return slots

    def base_of(p):
        return p // 4 * 16 + p % 4 * 2

    def pair_rows(base):
        a, b = qg_ref[base], qg_ref[base + 1]
        zero = jnp.zeros_like(a)
        return jnp.concatenate(
            [jnp.concatenate([a, zero], axis=1), jnp.concatenate([zero, b], axis=1)], axis=0
        )

    def pair_keys(slots, offset):
        return jnp.concatenate(
            [
                jnp.concatenate([kv_ref[slots[j] + offset], kv_ref[slots[8 + j] + offset]], axis=1)
                for j in range(8)
            ],
            axis=0,
        )

    def score(p, s_ref, w_ref):
        slots, base = slots_of(p), base_of(p)
        s_ref[...] = dot(pair_keys(slots, 0), pair_rows(base), NT)
        w_ref[...] = dot(pair_keys(slots, 8), pair_rows(base + 8), NT)

    def soften(p, s_ref, w_ref, d_ref, p_ref):
        low = jnp.where(first & (block_of(p) == 0), -jnp.inf, 0.0)
        high = jnp.where(~first & (block_of(p) == 254), -jnp.inf, 0.0)
        s = s_ref[...] * SCALE_LOG2E
        s = jnp.concatenate(
            [s[:BS] + low, s[BS : 2 * BS], s[2 * BS : 3 * BS] + high, s[3 * BS :]], axis=0
        )
        e = jnp.exp2(s - jnp.max(s, axis=0, keepdims=True))
        weights = e * (1.0 / jnp.sum(e, axis=0, keepdims=True))
        p_ref[...] = weights.astype(jnp.bfloat16)
        rd = rd_ref[p // 4, pl.ds(half + p % 4, 1), :]
        d_ref[...] = (weights * (w_ref[...] - rd)).astype(jnp.bfloat16)

    def spread(p, d_ref, p_ref):
        slots, base = slots_of(p), base_of(p)
        d = d_ref[...]
        dq = dot(d, pair_keys(slots, 0), TN) * SCALE
        dq_ref[2 * p] = dq[:BS, :DH].astype(jnp.bfloat16)
        dq_ref[2 * p + 1] = dq[BS:, DH:].astype(jnp.bfloat16)
        dk = dot(d, pair_rows(base), NN)
        dv = dot(p_ref[...], pair_rows(base + 8), NN)
        for j in range(16):
            side, row = j // 8 * DH, j % 8 * BS
            acc_ref[slots[j]] += dk[row : row + BS, side : side + DH]
            acc_ref[slots[j] + 8] += dv[row : row + BS, side : side + DH]

    score(0, s0, w0)
    soften(0, s0, w0, d0, p0)
    score(1, s1, w1)

    @pl.loop(1, 16)
    def _(t):
        a = 2 * t
        spread(a - 2, d0, p0)
        soften(a - 1, s1, w1, d1, p1)
        score(a, s0, w0)
        spread(a - 1, d1, p1)
        soften(a, s0, w0, d0, p0)
        score(a + 1, s1, w1)

    soften(31, s1, w1, d1, p1)
    spread(30, d0, p0)
    spread(31, d1, p1)


def attend(rand, glob, qg, rd, kv, zeros):
    vmem = pl.BlockSpec(memory_space=pltpu.VMEM)
    smem = pl.BlockSpec(memory_space=pltpu.SMEM)
    return pl.pallas_call(
        attend_kernel,
        out_shape=(
            jax.ShapeDtypeStruct((64, BS, DH), jnp.bfloat16),
            jax.ShapeDtypeStruct((512, BS, DH), jnp.float32),
        ),
        in_specs=[smem, smem, vmem, vmem, vmem, vmem],
        out_specs=(vmem, vmem),
        input_output_aliases={5: 1},
        scratch_shapes=[pltpu.VMEM((8 * BS, 2 * BS), jnp.float32)] * 4
        + [pltpu.VMEM((8 * BS, 2 * BS), jnp.bfloat16)] * 4,
        compiler_params=pltpu.CompilerParams(vmem_limit_bytes=ATTEND_VMEM),
    )(
        *(pltpu.with_memory_space_constraint(a, pltpu.MemorySpace.HBM) for a in (rand, glob)),
        qg,
        rd,
        kv,
        zeros,
    )


def on_device(
    queries, key_states, value_states, forward_out, grad_out, random_blocks, global_blocks
):
    kv, qg, rd, zeros = fetch(key_states, value_states, queries, grad_out, forward_out)
    dq, acc = attend(
        random_blocks.transpose(2, 1, 0),
        global_blocks,
        qg.reshape(128, BS, DH),
        rd,
        kv.reshape(512, BS, DH),
        zeros,
    )
    outs = give(dq.reshape(8, 512, DH), acc.reshape(32, 2, 512, DH))
    return outs[0], outs[1], outs[2]


def solution(mesh):
    return jax.shard_map(
        on_device,
        mesh=mesh,
        in_specs=(
            P("seq", "head"),
            P("seq", "head"),
            P("seq", "head"),
            P("seq", "head"),
            P("seq", "head"),
            P(None, "head", None),
            P(),
        ),
        out_specs=(P(("seq", "head"), None), P(("seq", "head"), None), P(("seq", "head"), None)),
        check_vma=False,
    )
```

```python
import jax
import jax.numpy as jnp
from jax import lax
from jax.experimental import pallas as pl
from jax.experimental.pallas import tpu as pltpu
from jax.sharding import PartitionSpec as P

DH = 128
BS = 64
SCALE = DH**-0.5
SCALE_LOG2E = SCALE * 1.4426950408889634
ATTEND_VMEM = 8 * 1024 * 1024
FETCH_VMEM = 10 * 1024 * 1024
GIVE_VMEM = 20 * 1024 * 1024
NT = (((1,), (1,)), ((), ()))
TN = (((0,), (0,)), ((), ()))
NN = (((1,), (0,)), ((), ()))


def dot(a, b, dims):
    return lax.dot_general(a, b, dims, preferred_element_type=jnp.float32)


MESH = pl.DeviceIdType.MESH


def index(z, x, c):
    return z * 8 + x % 4 * 2 + c


class Mover:
    def __init__(self, send, local):
        self.send, self.local = send, local
        self.sent, self.moved = [], []

    def push(self, src, dst, sem, peer):
        copy = pltpu.make_async_remote_copy(
            src_ref=src,
            dst_ref=dst,
            send_sem=self.send.at[len(self.sent)],
            recv_sem=sem,
            device_id=peer,
            device_id_type=MESH,
        )
        copy.start()
        self.sent.append(copy)

    def arrived(self, dst, sem, peer):
        pltpu.make_async_remote_copy(
            src_ref=dst,
            dst_ref=dst,
            send_sem=self.send.at[0],
            recv_sem=sem,
            device_id=peer,
            device_id_type=MESH,
        ).wait_recv()

    def move(self, src, dst):
        copy = pltpu.make_async_copy(src, dst, self.local.at[len(self.moved)])
        copy.start()
        self.moved.append(copy)
        return copy


def welcome(peers):
    barrier = pltpu.get_barrier_semaphore()
    for peer in peers:
        pl.semaphore_signal(barrier, inc=1, device_id=peer, device_id_type=MESH)


def enter(peers):
    pl.semaphore_wait(pltpu.get_barrier_semaphore(), len(peers))


def fetch_kernel(
    k_ref, v_ref, q_ref, g_ref, o_ref,
    kv_out, qg_out, rd_out, zeros,
    oth, rd_mine, g_all, o_all,
    send, local, from_x, from_pair, from_mirror, from_core, from_rd,
):
    s = lax.axis_index("seq")
    z, x, c = s // 8, s // 2 % 4, s % 2
    zhi = z // 2
    mirror, pair, core = 3 - z, z + 1 - 2 * (z % 2), 1 - c
    to_mirror = {"seq": index(mirror, x, c)}
    to_pair = {"seq": index(pair, x, c)}
    to_core = {"seq": index(z, x, core)}
    along_x = [{"seq": index(z, x + d, c)} for d in range(4)]
    mover = Mover(send, local)
    push, move = mover.push, mover.move

    def arrived(dst, sem):
        mover.arrived(dst, sem, to_core)

    ins = (k_ref, v_ref, q_ref, g_ref)

    def head(a, xx, half):
        return ins[a].at[:, pl.ds(pl.multiple_of(xx % 4 * 256 + half * DH, DH), DH)]

    def send_own(d, a):
        dst = kv_out.at[s, a] if a < 2 else qg_out.at[x, a - 2]
        push(head(a, x + d, zhi), dst, from_x.at[d - 1, a, 0], along_x[d])

    def send_other(d, a):
        push(head(a, x + d, 1 - zhi), oth.at[x, a], from_x.at[d - 1, a, 1], along_x[d])

    def at(zz, r, a, cc=c):
        return kv_out.at[index(zz, x + r, cc), a]

    def forward(src, dst, m, r, a):
        push(src, dst, from_pair.at[m, r, a], to_pair)
        push(src, dst, from_core.at[m, r, a], to_core)

    def own(r, a):
        piece = at(z, r, a)
        arrived(piece, from_x.at[3 - r, a, 0])
        forward(piece, piece, 0, r, a)

    def other(r, a):
        src = (x + r) % 4
        arrived(oth.at[src, a], from_x.at[3 - r, a, 1])
        dst = at(z, r, a) if a < 2 else qg_out.at[4 + src, a - 2]
        push(oth.at[src, a], dst, from_mirror.at[r, a], to_mirror)

    def mirrored(r, a):
        piece = at(mirror, r, a)
        arrived(piece, from_mirror.at[r, a])
        forward(piece, piece, 1, r, a)

    def paired(m, r, a):
        piece = at(3 - pair if m else pair, r, a)
        arrived(piece, from_pair.at[m, r, a])
        push(piece, piece, from_core.at[2 + m, r, a], to_core)

    dots = [move(g_ref, g_all), move(o_ref, o_all)]
    welcome(along_x[1:] + [to_mirror, to_pair, to_core])
    enter(along_x[1:] + [to_mirror, to_pair, to_core])
    for a in (0, 1):
        push(head(a, x, zhi), at(z, 0, a), from_pair.at[0, 0, a], to_pair)
        push(head(a, x, 1 - zhi), at(z, 0, a), from_mirror.at[0, a], to_mirror)
        send_own(1, a)
        send_own(3, a)
    for a in (0, 1):
        send_other(1, a)
        send_other(3, a)
        push(head(a, x, zhi), at(z, 0, a), from_core.at[0, 0, a], to_core)
    stores = [move(head(a, x, zhi), at(z, 0, a)) for a in (0, 1)]
    stores += [move(head(a, x, zhi), qg_out.at[x, a - 2]) for a in (2, 3)]
    for a in (0, 1):
        send_other(2, a)
    for a in (0, 1):
        send_own(2, a)
    for a in (2, 3):
        push(head(a, x, 1 - zhi), qg_out.at[4 + x, a - 2], from_mirror.at[0, a], to_mirror)
    for load in dots:
        load.wait()
    ones = jnp.ones((16, 2 * DH), jnp.bfloat16)
    for h in range(8):
        cols = slice(h * DH, (h + 1) * DH)
        terms = g_all[:, cols].astype(jnp.float32) * o_all[:, cols].astype(jnp.float32)
        high = terms.astype(jnp.bfloat16)
        low = (terms - high.astype(jnp.float32)).astype(jnp.bfloat16)
        sums = dot(ones, jnp.concatenate([high, low], axis=1), NT)
        for t in range(4):
            rd_mine[h // 2, h % 2 * 4 + t : h % 2 * 4 + t + 1, :] = sums[
                0:1, t * 128 : (t + 1) * 128
            ]
    own(3, 0)
    own(1, 0)
    mirrored(0, 0)
    own(3, 1)
    own(1, 1)
    mirrored(0, 1)
    rd_load = move(rd_mine.at[x], rd_out.at[x])
    for d in (1, 2, 3):
        push(rd_mine.at[(x + d) % 4], rd_out.at[x], from_rd.at[d], along_x[d])
    for d in (1, 3, 2):
        for a in (2, 3):
            send_other(d, a)
    for d in (2, 1, 3):
        for a in (2, 3):
            send_own(d, a)
    other(3, 0)
    other(1, 0)
    paired(0, 0, 0)
    paired(0, 0, 1)
    other(3, 1)
    other(1, 1)
    paired(0, 3, 0)
    paired(0, 1, 0)
    mirrored(3, 0)
    other(2, 0)
    mirrored(1, 0)
    other(2, 1)
    paired(1, 0, 0)
    paired(0, 3, 1)
    mirrored(3, 1)
    paired(0, 1, 1)
    own(2, 0)
    mirrored(1, 1)
    own(2, 1)
    mirrored(2, 0)
    paired(1, 0, 1)
    other(3, 2)
    other(1, 2)
    mirrored(2, 1)
    other(3, 3)
    other(1, 3)
    rd_load.wait()
    for d in (1, 2, 3):
        arrived(rd_out.at[(x + 4 - d) % 4], from_rd.at[d])
    near, far = pl.ds(0, 4), pl.ds(4, 4)
    push(rd_out.at[near], rd_out.at[far], from_rd.at[0], to_mirror)
    paired(1, 3, 0)
    paired(1, 1, 0)
    other(2, 2)
    other(2, 3)

    @pl.loop(0, 32)
    def _(i):
        zeros[pl.ds(i * 16, 16)] = jnp.zeros((16, BS, DH), jnp.float32)

    paired(1, 3, 1)
    paired(0, 2, 0)
    paired(1, 1, 1)
    paired(0, 2, 1)
    paired(1, 2, 0)
    paired(1, 2, 1)
    for r in (3, 1, 2):
        for a in (2, 3):
            arrived(qg_out.at[(x + r) % 4, a - 2], from_x.at[3 - r, a, 0])
    for r in range(4):
        for a in (0, 1):
            arrived(qg_out.at[4 + (x + r) % 4, a], from_mirror.at[r, 2 + a])
            for m, zz in enumerate((z, mirror, pair, 3 - pair)):
                arrived(at(zz, r, a, core), from_core.at[m, r, a])
    arrived(rd_out.at[far], from_rd.at[0])
    for copy in stores:
        copy.wait()
    for copy in mover.sent:
        copy.wait_send()


def fetch(k, v, q, g, o):
    anywhere = pl.BlockSpec(memory_space=pl.ANY)
    vmem = pl.BlockSpec(memory_space=pltpu.VMEM)
    dma = pltpu.SemaphoreType.DMA
    return pl.pallas_call(
        fetch_kernel,
        out_shape=(
            jax.ShapeDtypeStruct((32, 2, 512, DH), jnp.bfloat16),
            jax.ShapeDtypeStruct((8, 2, 512, DH), jnp.bfloat16),
            jax.ShapeDtypeStruct((8, 8, 128), jnp.float32),
            jax.ShapeDtypeStruct((512, BS, DH), jnp.float32),
        ),
        in_specs=[pl.BlockSpec(memory_space=pltpu.MemorySpace.HBM)] * 5,
        out_specs=(anywhere, anywhere, vmem, vmem),
        scratch_shapes=[
            pltpu.VMEM((4, 4, 512, DH), jnp.bfloat16),
            pltpu.VMEM((4, 8, 128), jnp.float32),
            pltpu.VMEM((512, 1024), jnp.bfloat16),
            pltpu.VMEM((512, 1024), jnp.bfloat16),
            dma((96,)),
            dma((7,)),
            dma((3, 4, 2)),
            dma((2, 4, 2)),
            dma((4, 4)),
            dma((4, 4, 2)),
            dma((4,)),
        ],
        compiler_params=pltpu.CompilerParams(
            collective_id=0, has_side_effects=True, vmem_limit_bytes=FETCH_VMEM
        ),
    )(*(pltpu.with_memory_space_constraint(a, pltpu.MemorySpace.HBM) for a in (k, v, q, g, o)))


def give_kernel(
    dq_ref, acc_ref, out_ref,
    part, away, near, far,
    send, local, from_core, from_pair, from_last, from_all,
):
    s = lax.axis_index("seq")
    y = lax.axis_index("head")
    z, x, c = s // 8, s // 2 % 4, s % 2
    zhi = z // 2
    mirror, pair, core = 3 - z, z + 1 - 2 * (z % 2), 1 - c
    to_pair = {"seq": index(pair, x, c), "head": y}
    to_core = {"seq": index(z, x, core), "head": y}
    order = (2, 1, 3, 0)

    def owner(m, r, t):
        return {"seq": index(mirror if m else z, x + r, c), "head": (y + t) % 4}

    peers = [
        owner(m, r, t) for m in (0, 1) for r in range(4) for t in range(4) if (m, r, t) != (0, 0, 0)
    ]
    mover = Mover(send, local)
    push, move = mover.push, mover.move
    classes = (3 - pair, pair, mirror, z)
    units = [(cls, r, a) for cls in range(4) for r in order for a in (0, 1)]
    kept = []

    def quarter(t):
        return pl.ds(pl.multiple_of((y + t) % 4 * 128, 128), 128)

    def hand(m, r, t, src, kind):
        col = pl.ds(pl.multiple_of(y * 1024 + (x * 2 + zhi) * DH, DH), DH)
        piece, dst = src.at[quarter(t)], out_ref.at[kind, :, col]
        if (m, r, t) == (0, 0, 0):
            kept.append(move(piece, dst))
        else:
            push(piece, dst, from_all.at[kind, m, r, t], owner(m, r, t))

    def spread(m, r, src, kind):
        for t in order:
            hand(m, r, t, src, kind)

    def add_rows(dst, slot, a, rows, terms):
        total = acc_ref[slot, a, rows, :]
        if a == 0:
            total *= SCALE
        for term in terms:
            total += term[rows, :].astype(jnp.float32)
        dst[rows, :] = total.astype(jnp.bfloat16)

    def add(dst, slot, a, terms):
        @pl.loop(0, 4)
        def _(i):
            rows = pl.ds(pl.multiple_of(i * 128, 128), 128)
            add_rows(dst, slot, a, rows, terms)

    def leave(cls, r, a):
        add(away.at[cls, r, a], index(classes[cls], x + r, core), a, ())

    def cross(cls, r, a):
        sem = from_core.at[cls, r, a]
        push(away.at[cls, r, a], near.at[cls, r, a], sem, to_core)

    welcome([to_core, to_pair] + peers)
    for unit in units[:16]:
        leave(*unit)
    enter([to_core, to_pair] + peers)
    for unit in units[:16]:
        cross(*unit)
    for cls, r, a in units[:14]:
        mover.arrived(near.at[cls, r, a], from_core.at[cls, r, a], to_core)
        mine = part.at[cls, r, a]
        add(mine, index(classes[cls], x + r, c), a, (near.at[cls, r, a],))
        push(mine, far.at[cls, r, a], from_pair.at[cls, r, a], to_pair)
        if (cls, r, a) == units[3]:
            for m in (1, 0):
                for rr in order:
                    spread(m, rr, dq_ref.at[m * 4 + (x + rr) % 4], 0)
            for unit in units[16:]:
                leave(*unit)
                cross(*unit)
    for a in (0, 1):
        mover.arrived(near.at[1, 0, a], from_core.at[1, 0, a], to_core)
    for t in order:
        for a in (0, 1):
            mine, rows = part.at[1, 0, a], quarter(t)
            add_rows(mine, index(pair, x, c), a, rows, (near.at[1, 0, a],))
            push(mine.at[rows], far.at[1, 0, a, rows], from_last.at[a, t], to_pair)
    for cls, r, a in units[16:30]:
        mover.arrived(near.at[cls, r, a], from_core.at[cls, r, a], to_core)
        mover.arrived(far.at[cls - 2, r, a], from_pair.at[cls - 2, r, a], to_pair)
        mine = part.at[cls, r, a]
        terms = (near.at[cls, r, a], far.at[cls - 2, r, a])
        add(mine, index(classes[cls], x + r, c), a, terms)
        spread(3 - cls, r, mine, 1 + a)
    for a in (0, 1):
        mover.arrived(near.at[3, 0, a], from_core.at[3, 0, a], to_core)
    for t in order:
        for a in (0, 1):
            mine, rows = part.at[3, 0, a], quarter(t)
            mover.arrived(far.at[1, 0, a, rows], from_last.at[a, t], to_pair)
            add_rows(mine, index(z, x, c), a, rows, (near.at[3, 0, a], far.at[1, 0, a]))
            hand(0, 0, t, mine, 1 + a)
    for m in (0, 1):
        for r in range(4):
            for t in range(4):
                if (m, r, t) == (0, 0, 0):
                    continue
                from_head = (x + 4 - r) % 4 * 2 + (1 - zhi if m else zhi)
                col = pl.multiple_of((y + 4 - t) % 4 * 1024 + from_head * DH, DH)
                for kind in range(3):
                    piece = out_ref.at[kind, :, pl.ds(col, DH)]
                    mover.arrived(piece, from_all.at[kind, m, r, t], to_core)
    for copy in kept:
        copy.wait()
    for copy in mover.sent:
        copy.wait_send()


def give(dq, acc):
    anywhere = pl.BlockSpec(memory_space=pl.ANY)
    dma = pltpu.SemaphoreType.DMA
    return pl.pallas_call(
        give_kernel,
        out_shape=jax.ShapeDtypeStruct((3, 128, 4096), jnp.bfloat16),
        in_specs=[anywhere, pl.BlockSpec(memory_space=pltpu.VMEM)],
        out_specs=anywhere,
        scratch_shapes=[
            pltpu.VMEM((4, 4, 2, 512, DH), jnp.bfloat16),
            pltpu.VMEM((4, 4, 2, 512, DH), jnp.bfloat16),
            pltpu.VMEM((4, 4, 2, 512, DH), jnp.bfloat16),
            pltpu.VMEM((2, 4, 2, 512, DH), jnp.bfloat16),
            dma((148,)),
            dma((3,)),
            dma((4, 4, 2)),
            dma((2, 4, 2)),
            dma((2, 4)),
            dma((3, 2, 4, 4)),
        ],
        compiler_params=pltpu.CompilerParams(
            collective_id=1, has_side_effects=True, vmem_limit_bytes=GIVE_VMEM
        ),
    )(dq, acc)


def attend_kernel(
    rand, glob, qg_ref, rd_ref, kv_ref, zeros_ref, dq_ref, acc_ref,
    s0, s1, w0, w1, d0, d1, p0, p1,
):
    s = lax.axis_index("seq")
    z, x, c = s // 8, s // 2 % 4, s % 2
    head = x * 2 + z // 2
    first = lax.broadcasted_iota(jnp.int32, (1, 2 * BS), 1) < BS
    half = z // 2 * 4

    def block_of(p):
        shard = jnp.where(p < 16, z, 3 - z) * 8 + p // 4 % 4 * 2 + c
        return shard * 8 + p % 4 * 2

    def slots_of(p):
        slots = []
        for block in (block_of(p), block_of(p) + 1):
            named = [jnp.maximum(block - 1, 0), block, jnp.minimum(block + 1, 255)]
            named += [rand[j, head, block] for j in range(3)] + [glob[0], glob[1]]
            slots += [2 * b - b % 8 for b in named]
        return slots

    def base_of(p):
        return p // 4 * 16 + p % 4 * 2

    def pair_rows(base):
        a, b = qg_ref[base], qg_ref[base + 1]
        zero = jnp.zeros_like(a)
        return jnp.concatenate(
            [jnp.concatenate([a, zero], axis=1), jnp.concatenate([zero, b], axis=1)], axis=0
        )

    def pair_keys(slots, offset):
        return jnp.concatenate(
            [
                jnp.concatenate([kv_ref[slots[j] + offset], kv_ref[slots[8 + j] + offset]], axis=1)
                for j in range(8)
            ],
            axis=0,
        )

    def score(p, s_ref, w_ref):
        slots, base = slots_of(p), base_of(p)
        s_ref[...] = dot(pair_keys(slots, 0), pair_rows(base), NT)
        w_ref[...] = dot(pair_keys(slots, 8), pair_rows(base + 8), NT)

    def soften(p, s_ref, w_ref, d_ref, p_ref):
        low = jnp.where(first & (block_of(p) == 0), -jnp.inf, 0.0)
        high = jnp.where(~first & (block_of(p) == 254), -jnp.inf, 0.0)
        s = s_ref[...] * SCALE_LOG2E
        s = jnp.concatenate(
            [s[:BS] + low, s[BS : 2 * BS], s[2 * BS : 3 * BS] + high, s[3 * BS :]], axis=0
        )
        e = jnp.exp2(s - jnp.max(s, axis=0, keepdims=True))
        weights = e * (1.0 / jnp.sum(e, axis=0, keepdims=True))
        p_ref[...] = weights.astype(jnp.bfloat16)
        rd = rd_ref[p // 4, pl.ds(half + p % 4, 1), :]
        d_ref[...] = (weights * (w_ref[...] - rd)).astype(jnp.bfloat16)

    def spread(p, d_ref, p_ref):
        slots, base = slots_of(p), base_of(p)
        d = d_ref[...]
        dq = dot(d, pair_keys(slots, 0), TN) * SCALE
        dq_ref[2 * p] = dq[:BS, :DH].astype(jnp.bfloat16)
        dq_ref[2 * p + 1] = dq[BS:, DH:].astype(jnp.bfloat16)
        dk = dot(d, pair_rows(base), NN)
        dv = dot(p_ref[...], pair_rows(base + 8), NN)
        for j in range(16):
            side, row = j // 8 * DH, j % 8 * BS
            acc_ref[slots[j]] += dk[row : row + BS, side : side + DH]
            acc_ref[slots[j] + 8] += dv[row : row + BS, side : side + DH]

    score(0, s0, w0)
    soften(0, s0, w0, d0, p0)
    score(1, s1, w1)

    @pl.loop(1, 16)
    def _(t):
        a = 2 * t
        spread(a - 2, d0, p0)
        soften(a - 1, s1, w1, d1, p1)
        score(a, s0, w0)
        spread(a - 1, d1, p1)
        soften(a, s0, w0, d0, p0)
        score(a + 1, s1, w1)

    soften(31, s1, w1, d1, p1)
    spread(30, d0, p0)
    spread(31, d1, p1)


def attend(rand, glob, qg, rd, kv, zeros):
    vmem = pl.BlockSpec(memory_space=pltpu.VMEM)
    smem = pl.BlockSpec(memory_space=pltpu.SMEM)
    return pl.pallas_call(
        attend_kernel,
        out_shape=(
            jax.ShapeDtypeStruct((64, BS, DH), jnp.bfloat16),
            jax.ShapeDtypeStruct((512, BS, DH), jnp.float32),
        ),
        in_specs=[smem, smem, vmem, vmem, vmem, vmem],
        out_specs=(vmem, vmem),
        input_output_aliases={5: 1},
        scratch_shapes=[pltpu.VMEM((8 * BS, 2 * BS), jnp.float32)] * 4
        + [pltpu.VMEM((8 * BS, 2 * BS), jnp.bfloat16)] * 4,
        compiler_params=pltpu.CompilerParams(vmem_limit_bytes=ATTEND_VMEM),
    )(
        *(pltpu.with_memory_space_constraint(a, pltpu.MemorySpace.HBM) for a in (rand, glob)),
        qg,
        rd,
        kv,
        zeros,
    )


def on_device(
    queries, key_states, value_states, forward_out, grad_out, random_blocks, global_blocks
):
    kv, qg, rd, zeros = fetch(key_states, value_states, queries, grad_out, forward_out)
    dq, acc = attend(
        random_blocks.transpose(2, 1, 0),
        global_blocks,
        qg.reshape(128, BS, DH),
        rd,
        kv.reshape(512, BS, DH),
        zeros,
    )
    outs = give(dq.reshape(8, 512, DH), acc.reshape(32, 2, 512, DH))
    return outs[0], outs[1], outs[2]


def solution(mesh):
    return jax.shard_map(
        on_device,
        mesh=mesh,
        in_specs=(
            P("seq", "head"),
            P("seq", "head"),
            P("seq", "head"),
            P("seq", "head"),
            P("seq", "head"),
            P(None, "head", None),
            P(),
        ),
        out_specs=(P(("seq", "head"), None), P(("seq", "head"), None), P(("seq", "head"), None)),
        check_vma=False,
    )
```
